256 devices in a mesh: gx: 32 (over y, z_lo, core), gy: 8 (over z_hi, x).
Axes of the slice: x: 4, y: 4, z: 8 (z_hi: 2, z_lo: 4; z = z_hi * 4 + z_lo), core: 2. Of those that a mesh axis runs over, the one named last changes fastest.
Arguments:
- tokens: bfloat16 [256, 64, 6144], P('gx', 'gy'), may hold values from -6 to 6
- upstream: bfloat16 [256, 64, 6144], P('gx', 'gy'), may hold values from -16 to 16
- gain_one: float32 [96], replicated, may hold values from 0.1 to 1.9
- gain_two: float32 [96], replicated, may hold values from 0.1 to 1.9
- attn_weight: bfloat16 [96, 288], replicated, may hold values from -2 to 2
- proj_weight: bfloat16 [96, 96], replicated, may hold values from -0.625 to 0.625
- expand_weight: bfloat16 [96, 384], replicated, may hold values from -0.625 to 0.625
- reduce_weight: bfloat16 [384, 96], replicated, may hold values from -0.3125 to 0.3125
Outputs:
- grad_tokens: bfloat16 [256, 64, 6144], P('gx', 'gy')
- grad_gain_one: float32 [96], replicated
- grad_gain_two: float32 [96], replicated
- grad_attn: float32 [96, 288], replicated
- grad_proj: float32 [96, 96], replicated
- grad_expand: float32 [96, 384], replicated
- grad_reduce: float32 [384, 96], replicated
The draws below stay inside these ranges and needn't reach their ends.
All inputs are finite; a program needn't handle non-finite values.
Results may differ from the reference program's by a relative error of at most 0.023.
The reference program's roundings to bfloat16 on the way count: a program that leaves them out, or rounds other values in their place, can miss the bound.
Values may be sent and summed in bfloat16 or wider, within the bound.
A program may use at most 128 MiB of HBM per device.

```python
import math
import jax
import jax.numpy as jnp
from jax import lax

D = 96
HEADS = 3
HID = 384
WIN = 8
NZ = 64
NX = 256
NY = 64
TOKENS = 1048576


def draw_attn_weight(key, part):
    drawn = jax.random.normal(key, (D, 3 * D), jnp.float32) / math.sqrt(D)
    return jnp.clip(drawn, -2.0, 2.0).astype(jnp.bfloat16)


def draw_upstream(key, part):
    place = jnp.arange(NX, dtype=jnp.float32) / max(NX - 1, 1)
    noise = jnp.clip(jax.random.normal(key, (NX, NY, NZ * D), jnp.float32), -6.0, 6.0)
    scale = 0.5 * jnp.exp(place * math.log(5.0))
    return (noise * scale[:, None, None]).astype(jnp.bfloat16)


def shard_levels(rng, dims, pieces, least, largest):
    def one(dim, shards_of):
        heights = jax.random.uniform(jax.random.fold_in(jax.random.fold_in(rng, 6), dim), (shards_of,), jnp.float32, least / len(pieces), largest / len(pieces))
        return jnp.repeat(jnp.exp(heights), dims[dim] // shards_of).reshape((-1,) + (1,) * (len(dims) - dim - 1))

    level = one(*pieces[0])
    for cut in pieces[1:]:
        level = level * one(*cut)
    return level


def normal_values(rng, shape, scale, most, shards=(), held_as=jnp.bfloat16):
    result = jax.random.normal(rng, shape, jnp.float32) * scale
    if len(shards) > 0:
        result = shard_levels(rng, shape, shards, -0.22, 0.18) * result
    return jnp.clip(result, min=-most, max=most).astype(held_as)


def setup_inputs(seed: int = 0) -> dict:
    seeds = jax.random.split(jax.random.key(seed), 9)
    tokens = normal_values(seeds[0], (NX, NY, NZ * D), 1.0, 6.0, ((0, 32), (1, 8)))
    upstream = draw_upstream(jax.random.fold_in(seeds[8], 71), 0)
    gain_one = jnp.clip(1.0 + 0.18 * jax.random.normal(seeds[2], (D,), jnp.float32), 0.1, 1.9)
    gain_two = jnp.clip(1.0 + 0.18 * jax.random.normal(seeds[3], (D,), jnp.float32), 0.1, 1.9)
    attn_weight = draw_attn_weight(jax.random.fold_in(seeds[8], 71), 0)
    proj_weight = normal_values(seeds[5], (D, D), D ** -0.5, 0.625)
    expand_weight = normal_values(seeds[6], (D, HID), D ** -0.5, 0.625)
    reduce_weight = normal_values(seeds[7], (HID, D), HID ** -0.5, 0.3125)
    return dict(tokens=tokens, upstream=upstream, gain_one=gain_one, gain_two=gain_two, attn_weight=attn_weight, proj_weight=proj_weight, expand_weight=expand_weight, reduce_weight=reduce_weight)


epsilon = 1e-05

def norm_rows(row_data, gain_vec):
    centre = row_data - lax.optimization_barrier(jnp.mean(row_data, axis=-1, keepdims=True))
    inverse = lax.rsqrt(lax.optimization_barrier(jnp.mean(centre * centre, axis=-1, keepdims=True)) + epsilon)
    normed = centre * inverse
    return (normed * gain_vec, normed, inverse)

def norm_back(grad_out, normed, inverse, gain_vec):
    scaled = grad_out * gain_vec
    mean_one = lax.optimization_barrier(jnp.mean(scaled, axis=-1, keepdims=True))
    mean_two = lax.optimization_barrier(jnp.mean(scaled * normed, axis=-1, keepdims=True))
    return (inverse * (scaled - mean_one - normed * mean_two), lax.optimization_barrier(jnp.sum(grad_out * normed, axis=0)))

def to_windows(grid_four):
    ext_x, ext_y, ext_z, width = grid_four.shape
    split = grid_four.reshape(ext_x // WIN, WIN, ext_y // WIN, WIN, ext_z // WIN, WIN, width)
    return split.transpose(0, 2, 4, 1, 3, 5, 6).reshape(-1, WIN ** 3, width)

def from_windows(windows, ext_x, ext_y, ext_z):
    width = windows.shape[-1]
    split = windows.reshape(ext_x // WIN, ext_y // WIN, ext_z // WIN, WIN, WIN, WIN, width)
    return split.transpose(0, 3, 1, 4, 2, 5, 6).reshape(ext_x, ext_y, ext_z, width)

def split_heads(packed):
    length = packed.shape[0]
    return packed.reshape(length, 3, HEADS, D // HEADS).transpose(1, 2, 0, 3).astype(jnp.float32)

def window_probs(parts):
    factor = (D // HEADS) ** (-0.5)
    scores = jnp.einsum('hqd,hkd->hqk', parts[0], parts[1]) * factor
    weights = jnp.exp(scores - lax.optimization_barrier(jnp.max(scores, axis=-1, keepdims=True)))
    return (weights / lax.optimization_barrier(jnp.sum(weights, axis=-1, keepdims=True))).astype(jnp.bfloat16)

def attend(packed):
    length = packed.shape[0]
    parts = split_heads(packed)
    probs = window_probs(parts)
    mixed = jnp.einsum('hqk,hkd->hqd', probs.astype(jnp.float32), parts[2]).astype(jnp.bfloat16)
    return mixed.transpose(1, 0, 2).reshape(length, D)

def attend_back(items):
    packed, grad_mix = items
    length = packed.shape[0]
    factor = (D // HEADS) ** (-0.5)
    parts = split_heads(packed)
    probs = window_probs(parts).astype(jnp.float32)
    grad_heads = grad_mix.reshape(length, HEADS, D // HEADS).transpose(1, 0, 2).astype(jnp.float32)
    grad_probs = jnp.einsum('hqd,hkd->hqk', grad_heads, parts[2])
    grad_values = jnp.einsum('hqk,hqd->hkd', probs, grad_heads)
    grad_scores = probs * (grad_probs - lax.optimization_barrier(jnp.sum(grad_probs * probs, axis=-1, keepdims=True))) * factor
    grad_scores = grad_scores.astype(jnp.bfloat16).astype(jnp.float32)
    grad_queries = jnp.einsum('hqk,hkd->hqd', grad_scores, parts[1])
    grad_keys = jnp.einsum('hqk,hqd->hkd', grad_scores, parts[0])
    stacked = jnp.stack([grad_queries, grad_keys, grad_values])
    return stacked.transpose(2, 0, 1, 3).reshape(length, 3 * D).astype(jnp.bfloat16)

def mlp_back(items, gain_two, expand_weight, reduce_weight):
    resid_rows, grad_rows = items
    resid = resid_rows.astype(jnp.float32)
    h2f, normed, inverse = norm_rows(resid, gain_two)
    h2 = h2f.astype(jnp.bfloat16)
    pre_act = jnp.dot(h2, expand_weight, preferred_element_type=jnp.float32)
    act, gelu_back = jax.vjp(jax.nn.gelu, pre_act)
    act_b = act.astype(jnp.bfloat16)
    sum_reduce = jnp.dot(act_b.T, grad_rows, preferred_element_type=jnp.float32)
    grad_act = jnp.dot(grad_rows, reduce_weight.T, preferred_element_type=jnp.float32)
    grad_pre = gelu_back(grad_act)[0].astype(jnp.bfloat16)
    sum_expand = jnp.dot(h2.T, grad_pre, preferred_element_type=jnp.float32)
    grad_h2 = jnp.dot(grad_pre, expand_weight.T, preferred_element_type=jnp.float32)
    part_grad, sum_two = norm_back(grad_h2, normed, inverse, gain_two)
    return (grad_rows.astype(jnp.float32) + part_grad, sum_expand, sum_reduce, sum_two)

def reference(tokens, upstream, gain_one, gain_two, attn_weight, proj_weight, expand_weight, reduce_weight):
    half_win = WIN // 2
    grid_shape = (NX, NY, NZ, D)
    base = tokens.reshape(-1, D).astype(jnp.float32)
    h1f, normed_one, inverse_one = norm_rows(base, gain_one)
    h1 = h1f.astype(jnp.bfloat16)
    rolled = jnp.roll(h1.reshape(grid_shape), (-half_win, -half_win, -half_win), (0, 1, 2))
    rolled_flat = rolled.reshape(-1, D)
    packed = jnp.dot(rolled_flat, attn_weight, preferred_element_type=jnp.float32).astype(jnp.bfloat16)
    packed_win = to_windows(packed.reshape(NX, NY, NZ, 3 * D))
    mixed_win = lax.map(attend, packed_win)
    mixed = from_windows(mixed_win, NX, NY, NZ).reshape(-1, D)
    branch = jnp.dot(mixed, proj_weight, preferred_element_type=jnp.float32).astype(jnp.bfloat16)
    branch_back = jnp.roll(branch.reshape(grid_shape), (half_win, half_win, half_win), (0, 1, 2)).reshape(-1, D)
    resid = (base + branch_back.astype(jnp.float32)).astype(jnp.bfloat16)
    grad_rows = upstream.reshape(-1, D)
    blocks = 8
    outs = lax.map(lambda items: mlp_back(items, gain_two, expand_weight, reduce_weight), (resid.reshape(blocks, -1, D), grad_rows.reshape(blocks, -1, D)))
    grad_resid = outs[0].reshape(-1, D)
    sum_expand = lax.optimization_barrier(jnp.sum(outs[1], axis=0))
    sum_reduce = lax.optimization_barrier(jnp.sum(outs[2], axis=0))
    sum_two = lax.optimization_barrier(jnp.sum(outs[3], axis=0))
    grad_branch = grad_resid.astype(jnp.bfloat16).reshape(grid_shape)
    grad_branch = jnp.roll(grad_branch, (-half_win, -half_win, -half_win), (0, 1, 2)).reshape(-1, D)
    sum_proj = jnp.dot(mixed.T, grad_branch, preferred_element_type=jnp.float32)
    grad_mix = jnp.dot(grad_branch, proj_weight.T, preferred_element_type=jnp.float32).astype(jnp.bfloat16)
    grad_packed_win = lax.map(attend_back, (packed_win, to_windows(grad_mix.reshape(grid_shape))))
    grad_packed = from_windows(grad_packed_win, NX, NY, NZ).reshape(-1, 3 * D)
    sum_attn = jnp.dot(rolled_flat.T, grad_packed, preferred_element_type=jnp.float32)
    grad_in = jnp.dot(grad_packed, attn_weight.T, preferred_element_type=jnp.float32).astype(jnp.bfloat16)
    grad_h1 = jnp.roll(grad_in.reshape(grid_shape), (half_win, half_win, half_win), (0, 1, 2)).reshape(-1, D)
    part_grad, sum_one = norm_back(grad_h1.astype(jnp.float32), normed_one, inverse_one, gain_one)
    grad_tokens = (grad_resid + part_grad).astype(jnp.bfloat16).reshape(NX, NY, NZ * D)
    factor = 1.0 / jnp.sqrt(jnp.float32(TOKENS))
    return (grad_tokens, sum_one * factor, sum_two * factor, sum_attn * factor, sum_proj * factor, sum_expand * factor, sum_reduce * factor)
```

```python
import math

import jax
import jax.numpy as jnp
from jax import lax
from jax.experimental import pallas as pl
from jax.experimental.pallas import tpu as pltpu
from jax.sharding import PartitionSpec as P

D = 96
HEADS = 3
HD = 32
WIN = 8
HID = 384
TOK = 512
CH = 384
EPS = 1e-05
F32 = jnp.float32
BF = jnp.bfloat16
SCALE = HD**-0.5
LOG2E = 1.4426950408889634
GC = math.sqrt(2.0 / math.pi)


def nn(a, b):
    return lax.dot_general(a, b, (((1,), (0,)), ((), ())), preferred_element_type=F32)


def nt(a, b):
    return lax.dot_general(a, b, (((1,), (1,)), ((), ())), preferred_element_type=F32)


def wide(col):
    return jnp.concatenate([col] * (TOK // 128), axis=1)


def fold(v):
    return v[:, 0:128] + v[:, 128:256] + v[:, 256:384] + v[:, 384:512]


def mean0(v):
    return jnp.sum(v, axis=0, keepdims=True) * (1.0 / D)


def norm_cols(v, gain):
    c = v - mean0(v)
    r = lax.rsqrt(mean0(c * c) + EPS)
    n = c * r
    return n * gain, n, r


def norm_back(dh, n, r, gain):
    e = dh * gain
    return r * (e - mean0(e) - n * mean0(e * n))


def load_window(ref, lo, hi):
    a = ref[:, :, pl.ds(lo, CH)].astype(F32).reshape(64, CH)
    b = ref[:, :, pl.ds(hi, CH)].astype(F32).reshape(64, CH)
    t = jnp.concatenate([a, b], axis=0).T
    return jnp.concatenate([t[0:96], t[96:192], t[192:288], t[288:384]], axis=1)


def store_window(ref, lo, hi, v):
    t = jnp.concatenate([v[:, 128 * i : 128 * (i + 1)] for i in range(4)], axis=0).T
    ref[:, :, pl.ds(lo, CH)] = t[0:64].reshape(8, 8, CH).astype(BF)
    ref[:, :, pl.ds(hi, CH)] = t[64:128].reshape(8, 8, CH).astype(BF)


def only_head(v, h):
    zero = jnp.zeros((HD, v.shape[1]), v.dtype)
    rows = [v[HD * h : HD * (h + 1)] if i == h else zero for i in range(HEADS)]
    return jnp.concatenate(rows, axis=0)


def offsets(w):
    lo = pl.multiple_of((2 * w + 1) * CH, 128)
    hi = pl.multiple_of(lax.rem(2 * w + 2, 16) * CH, 128)
    return lo, hi


def kernel(
    x_ref, g_ref, gain1, gain2, wa, wat, wp, wpt, we, wet, wr,
    out_ref, s_red, s_exp, s_proj, s_two, s_attn, s_one,
    probs, packed, vnat, h1s, n1s, r1s, dy1s, dmixs, deltas,
):
    s_red[...] = jnp.zeros_like(s_red)
    s_exp[...] = jnp.zeros_like(s_exp)
    s_proj[...] = jnp.zeros_like(s_proj)
    s_two[...] = jnp.zeros_like(s_two)
    s_attn[...] = jnp.zeros_like(s_attn)
    s_one[...] = jnp.zeros_like(s_one)

    def front(w, carry):
        lo, hi = offsets(w)
        x = load_window(x_ref, lo, hi)
        h1f, n1, r1 = norm_cols(x, wide(gain1[...]))
        h1 = h1f.astype(BF)
        h1s[w] = h1
        n1s[w] = n1
        r1s[w] = jnp.broadcast_to(r1, (8, TOK))
        pk = nn(wat[...], h1).astype(BF)
        packed[w] = pk
        qt, vt = pk[0:96], pk[192:288]
        kn = pk[96:192].T
        vnat[w] = vt.T
        mixed = []
        for h in range(HEADS):
            qm = only_head(qt, h)
            parts = []
            for c in range(2):
                cols = slice(256 * c, 256 * (c + 1))
                s = nn(kn, qm[:, cols])
                m = jnp.max(s, axis=0, keepdims=True)
                e = jnp.exp2((s - m) * (SCALE * LOG2E))
                inv = 1.0 / jnp.sum(e, axis=0, keepdims=True)
                p = (e * inv).astype(BF)
                probs[w * HEADS + h, :, cols] = p
                parts.append(nn(vt[HD * h : HD * (h + 1)], p))
            mixed.append(jnp.concatenate(parts, axis=1))
        mixed_f = jnp.concatenate(mixed, axis=0)
        mixed = mixed_f.astype(BF)
        branch = nn(wpt[...], mixed).astype(BF)
        y1 = (x + branch.astype(F32)).astype(BF).astype(F32)
        gain_b = wide(gain2[...])
        h2f, n2, r2 = norm_cols(y1, gain_b)
        h2 = h2f.astype(BF)
        u = nn(wet[...], h2)
        u2 = u * u
        t = jnp.tanh(u * (GC + (GC * 0.044715) * u2))
        half = 0.5 + 0.5 * t
        act = (u * half).astype(BF)
        slope = half + (0.5 * u) * (1.0 - t * t) * (GC + (3 * 0.044715 * GC) * u2)
        gf = load_window(g_ref, lo, hi)
        gb = gf.astype(BF)
        s_red[...] += nt(gb, act)
        du = (nn(wr[...], gb) * slope).astype(BF)
        s_exp[...] += nt(h2, du)
        dh2 = nn(we[...], du)
        s_two[...] += fold(dh2 * n2)
        dy1 = gf + norm_back(dh2, n2, r2, gain_b)
        dy1s[w] = dy1
        da = dy1.astype(BF)
        s_proj[...] += nt(mixed, da)
        dmix = nn(wp[...], da).astype(BF)
        dmixs[w] = dmix
        prod = dmix.astype(F32) * mixed_f
        rows = [jnp.sum(prod[HD * h : HD * (h + 1)], axis=0, keepdims=True) for h in range(HEADS)]
        deltas[w] = jnp.concatenate(rows + [jnp.zeros((8 - HEADS, TOK), F32)], axis=0)
        return carry

    lax.fori_loop(0, 8, front, 0)

    def back(w, carry):
        lo, hi = offsets(w)
        pk = packed[w]
        qt, kt = pk[0:96], pk[96:192]
        vn = vnat[w]
        dmix = dmixs[w]
        delta = deltas[w]
        dqs, dks, dvs = [], [], []
        for h in range(HEADS):
            rows = slice(HD * h, HD * (h + 1))
            dm = only_head(dmix, h)
            dq, dk, dv = [], 0.0, 0.0
            for c in range(2):
                cols = slice(256 * c, 256 * (c + 1))
                p = probs[w * HEADS + h, :, cols]
                dp = nn(vn, dm[:, cols])
                ds = (p.astype(F32) * (dp - delta[h : h + 1, cols]) * SCALE).astype(BF)
                dq.append(nn(kt[rows], ds))
                dk = dk + nt(qt[rows, cols], ds)
                dv = dv + nt(dmix[rows, cols], p)
            dqs.append(jnp.concatenate(dq, axis=1))
            dks.append(dk)
            dvs.append(dv)
        dpk = jnp.concatenate(dqs + dks + dvs, axis=0).astype(BF)
        s_attn[...] += nt(h1s[w], dpk)
        dh1 = nn(wa[...], dpk).astype(BF).astype(F32)
        n1 = n1s[w]
        s_one[...] += fold(dh1 * n1)
        r1 = r1s[w][0:1]
        store_window(out_ref, lo, hi, dy1s[w] + norm_back(dh1, n1, r1, wide(gain1[...])))
        return carry

    lax.fori_loop(0, 8, back, 0)


def compute(x, g, gain_one, gain_two, attn_weight, proj_weight, expand_weight, reduce_weight):
    vm = pl.BlockSpec(memory_space=pltpu.VMEM)
    shape = jax.ShapeDtypeStruct
    col = lambda v: jnp.broadcast_to(v[:, None], (D, 128))
    return pl.pallas_call(
        kernel,
        in_specs=[vm] * 11,
        out_specs=[vm] * 7,
        out_shape=[
            shape((8, 8, 6144), BF),
            shape((D, HID), F32),
            shape((D, HID), F32),
            shape((D, D), F32),
            shape((D, 128), F32),
            shape((D, 3 * D), F32),
            shape((D, 128), F32),
        ],
        scratch_shapes=[
            pltpu.VMEM((24, TOK, TOK), BF),
            pltpu.VMEM((8, 3 * D, TOK), BF),
            pltpu.VMEM((8, TOK, D), BF),
            pltpu.VMEM((8, D, TOK), BF),
            pltpu.VMEM((8, D, TOK), F32),
            pltpu.VMEM((8, 8, TOK), F32),
            pltpu.VMEM((8, D, TOK), F32),
            pltpu.VMEM((8, D, TOK), BF),
            pltpu.VMEM((8, 8, TOK), F32),
        ],
        compiler_params=pltpu.CompilerParams(vmem_limit_bytes=56 * 1024 * 1024),
        name="block_backward",
    )(
        x, g, col(gain_one), col(gain_two),
        attn_weight, attn_weight.T, proj_weight, proj_weight.T,
        expand_weight, expand_weight.T, reduce_weight,
    )


def shifted(value, axis, steps):
    count = lax.axis_size(axis)
    return lax.ppermute(value, axis, [(s, (s + steps) % count) for s in range(count)])


def ahead(v):
    v = jnp.concatenate([v[4:], shifted(v[:4], "gx", -1)], axis=0)
    return jnp.concatenate([v[:, 4:], shifted(v[:, :4], "gy", -1)], axis=1)


def behind(v):
    v = jnp.concatenate([shifted(v[:, 4:], "gy", 1), v[:, :4]], axis=1)
    return jnp.concatenate([shifted(v[4:], "gx", 1), v[:4]], axis=0)


def local(tokens, upstream, gain_one, gain_two, attn_weight, proj_weight, expand_weight, reduce_weight):
    count = tokens.shape[0] * tokens.shape[1] * (tokens.shape[2] // D)
    factor = 1.0 / math.sqrt(count * lax.axis_size("gx") * lax.axis_size("gy"))
    outs = compute(
        ahead(tokens), ahead(upstream), gain_one, gain_two,
        attn_weight, proj_weight, expand_weight, reduce_weight,
    )
    grad = behind(outs[0])
    red, exp, proj, two, attn, one = lax.psum(
        (outs[1], outs[2], outs[3], jnp.sum(outs[4], axis=1), outs[5], jnp.sum(outs[6], axis=1)),
        ("gx", "gy"),
    )
    return (grad, one * factor, two * factor, attn * factor, proj * factor, exp * factor, red.T * factor)


def solution(mesh):
    return jax.shard_map(
        local,
        mesh=mesh,
        in_specs=(P("gx", "gy", None), P("gx", "gy", None), P(), P(), P(), P(), P(), P()),
        out_specs=(P("gx", "gy", None), P(), P(), P(), P(), P(), P()),
        check_vma=False,
    )
```

```python
import functools
import math

import jax
import jax.numpy as jnp
from jax import lax
from jax.experimental import pallas as pl
from jax.experimental.pallas import tpu as pltpu
from jax.sharding import PartitionSpec as P

D = 96
HEADS = 3
HD = 32
WIN = 8
HID = 384
TOK = 512
CH = 384
EPS = 1e-05
F32 = jnp.float32
BF = jnp.bfloat16
SCALE = HD**-0.5
LOG2E = 1.4426950408889634
GC = math.sqrt(2.0 / math.pi)


def nn(a, b):
    return lax.dot_general(a, b, (((1,), (0,)), ((), ())), preferred_element_type=F32)


def nt(a, b):
    return lax.dot_general(a, b, (((1,), (1,)), ((), ())), preferred_element_type=F32)


def wide(col):
    return jnp.concatenate([col] * (TOK // 128), axis=1)


def fold(v):
    return v[:, 0:128] + v[:, 128:256] + v[:, 256:384] + v[:, 384:512]


def mean0(v):
    return jnp.sum(v, axis=0, keepdims=True) * (1.0 / D)


def norm_cols(v, gain):
    c = v - mean0(v)
    r = lax.rsqrt(mean0(c * c) + EPS)
    n = c * r
    return n * gain, n, r


def norm_back(dh, n, r, gain):
    e = dh * gain
    return r * (e - mean0(e) - n * mean0(e * n))


def flip(v):
    return v.astype(F32).T.astype(v.dtype)


def load_window(ref, lo, hi):
    a = ref[:, :, pl.ds(lo, CH)].astype(F32).reshape(64, CH)
    b = ref[:, :, pl.ds(hi, CH)].astype(F32).reshape(64, CH)
    t = jnp.concatenate([a, b], axis=0).T
    return jnp.concatenate([t[0:96], t[96:192], t[192:288], t[288:384]], axis=1)


def store_window(ref, lo, hi, v):
    t = jnp.concatenate([v[:, 128 * i : 128 * (i + 1)] for i in range(4)], axis=0).T
    ref[:, :, pl.ds(lo, CH)] = t[0:64].reshape(8, 8, CH).astype(BF)
    ref[:, :, pl.ds(hi, CH)] = t[64:128].reshape(8, 8, CH).astype(BF)


def only_head(v, h):
    zero = jnp.zeros((HD, v.shape[1]), v.dtype)
    rows = [v[HD * h : HD * (h + 1)] if i == h else zero for i in range(HEADS)]
    return jnp.concatenate(rows, axis=0)


def offsets(w):
    lo = pl.multiple_of((2 * w + 1) * CH, 128)
    hi = pl.multiple_of(lax.rem(2 * w + 2, 16) * CH, 128)
    return lo, hi


MESH = pl.DeviceIdType.MESH
NGX, NGY = 32, 8
GROUP = 16
SHIFTS = ((1, 1), (0, 1), (1, 0))
CUTS = (0, 5 * CH, 11 * CH, 16 * CH)
READY = (0, 2, 5)
ROWS_A, ROWS_B = 48, 24


def half(flag):
    return pl.ds(4, 4) if flag else pl.ds(0, 4)


def place():
    a, b = lax.axis_index("gx"), lax.axis_index("gy")
    first = (b // 4) * 8 + lax.rem(a, 8)
    second = (a // 8) * 4 + lax.rem(b, 4)
    return a, b, first, second


def device(first, second):
    return ((second // 4) * 8 + lax.rem(first, 8), (first // 8) * 4 + lax.rem(second, 4))


def neighbour(dx, dy):
    a, b = lax.axis_index("gx"), lax.axis_index("gy")
    return (lax.rem(a + dx + NGX, NGX), lax.rem(b + dy + NGY, NGY))


def remote(src, dst, send, recv, where):
    return pltpu.make_async_remote_copy(
        src_ref=src, dst_ref=dst, send_sem=send, recv_sem=recv, device_id=where, device_id_type=MESH
    )


def halo_in(src, dst, send, recv, part, k):
    dx, dy = SHIFTS[k]
    cols = pl.ds(CUTS[part], CUTS[part + 1] - CUTS[part])
    return remote(
        src.at[half(not dx), half(not dy), cols], dst.at[half(dx), half(dy), cols],
        send.at[part, k], recv.at[part, k], neighbour(-dx, -dy),
    )


def own_in(src, dst, sem, part):
    cols = pl.ds(CUTS[part], CUTS[part + 1] - CUTS[part])
    return pltpu.make_async_copy(
        src.at[half(1), half(1), cols], dst.at[half(0), half(0), cols], sem.at[part]
    )


def halo_out(src, dst, send, recv, k, cols):
    dx, dy = SHIFTS[k]
    return remote(
        src.at[half(dx), half(dy), cols], dst.at[half(not dx), half(not dy), cols],
        send.at[k], recv.at[k], neighbour(dx, dy),
    )


def own_out(src, dst, sem, cols):
    return pltpu.make_async_copy(
        src.at[half(0), half(0), cols], dst.at[half(1), half(1), cols], sem
    )


def send_out(src, dst, send, recv, sem, cols):
    for k in range(3):
        halo_out(src, dst, send, recv, k, cols).start()
    own_out(src, dst, sem, cols).start()


def spread(src_of, dst, slot, send, recv, along_first):
    a, b, first, second = place()
    mine = first if along_first else second

    def step(r, carry):
        to = lax.rem(mine + r, GROUP)
        where = device(to, second) if along_first else device(first, to)
        remote(src_of(to), dst.at[slot], send, recv, where).start()
        return carry

    lax.fori_loop(1, GROUP, step, 0)


def settle(buf, send, recv):
    most = buf.at[pl.ds(0, GROUP - 1)]
    done = remote(most, most, send, recv, neighbour(1, 0))
    done.wait_recv()
    done.wait_send()


def total(buf):
    acc = buf[0]
    for i in range(1, GROUP):
        acc = acc + buf[i]
    return acc


def reduce_start(parts, got, sems):
    a, b, first, second = place()
    got[first] = parts[first]
    spread(lambda to: parts.at[to], got, first, sems.at[0, 0], sems.at[1, 0], True)


def reduce_middle(got, cross, sems, factor):
    a, b, first, second = place()
    settle(got, sems.at[0, 0], sems.at[1, 0])
    cross[second] = total(got) * factor
    spread(lambda to: cross.at[second], cross, second, sems.at[0, 1], sems.at[1, 1], False)


def reduce_last(cross, final, sems):
    a, b, first, second = place()
    settle(cross, sems.at[0, 1], sems.at[1, 1])
    final[first] = total(cross)
    spread(lambda to: final.at[first], final, first, sems.at[0, 2], sems.at[1, 2], True)


def reduce_end(final, sems):
    settle(final, sems.at[0, 2], sems.at[1, 2])


def kernel(
    factor, tok_ref, up_ref, gain1_ref, gain2_ref, wa, wp, we, wrt,
    out_ref, o_one, o_two, o_attn, o_proj, o_exp, o_red,
    rx, rg, ob, wat, wpt, wet, wr, gain1, gain2,
    s_red, s_exp, s_proj, s_two, s_attn, s_one,
    probs, packed, vnat, h1s, n1s, r1s, mixes, dy1s, dmixs, deltas,
    a_parts, a_got, a_cross, a_final, b_parts, b_got, b_cross, b_final,
    x_send, x_recv, g_send, g_recv, x_own, g_own, y_send, y_recv, y_own, a_sems, b_sems,
):
    a, b, first, second = place()
    barrier = pltpu.get_barrier_semaphore()
    for dx, dy in SHIFTS:
        for sign in (-1, 1):
            pl.semaphore_signal(
                barrier, inc=1, device_id=neighbour(sign * dx, sign * dy), device_id_type=MESH
            )

    def greet(r, carry):
        pl.semaphore_signal(
            barrier, inc=1, device_id=device(lax.rem(first + r, GROUP), second), device_id_type=MESH
        )
        pl.semaphore_signal(
            barrier, inc=1, device_id=device(first, lax.rem(second + r, GROUP)), device_id_type=MESH
        )
        return carry

    lax.fori_loop(1, GROUP, greet, 0)
    for part in range(3):
        own_in(tok_ref, rx, x_own, part).start()
        own_in(up_ref, rg, g_own, part).start()
    pl.semaphore_wait(barrier, 2 * len(SHIFTS) + 2 * (GROUP - 1))
    for part in range(3):
        for k in range(3):
            halo_in(tok_ref, rx, x_send, x_recv, part, k).start()
    for part in range(3):
        for k in range(3):
            halo_in(up_ref, rg, g_send, g_recv, part, k).start()

    wat[...] = flip(wa[...])
    wpt[...] = flip(wp[...])
    wet[...] = flip(we[...])
    wr[...] = flip(wrt[...])
    gain1[...] = jnp.broadcast_to(gain1_ref[...], (128, D)).T
    gain2[...] = jnp.broadcast_to(gain2_ref[...], (128, D)).T
    s_red[...] = jnp.zeros_like(s_red)
    s_exp[...] = jnp.zeros_like(s_exp)
    s_proj[...] = jnp.zeros_like(s_proj)
    s_two[...] = jnp.zeros_like(s_two)
    s_attn[...] = jnp.zeros_like(s_attn)
    s_one[...] = jnp.zeros_like(s_one)

    def attend(w, carry):
        for part in range(3):

            @pl.when(w == READY[part])
            def _(part=part):
                own_in(tok_ref, rx, x_own, part).wait()
                for k in range(3):
                    halo_in(tok_ref, rx, x_send, x_recv, part, k).wait_recv()

        lo, hi = offsets(w)
        x = load_window(rx, lo, hi)
        h1f, n1, r1 = norm_cols(x, wide(gain1[...]))
        h1 = h1f.astype(BF)
        h1s[w] = h1
        n1s[w] = n1
        r1s[w] = jnp.broadcast_to(r1, (8, TOK))
        pk = nn(wat[...], h1).astype(BF)
        packed[w] = pk
        qt, vt = pk[0:96], pk[192:288]
        kn = pk[96:192].T
        vnat[w] = vt.T
        mixed = []
        for h in range(HEADS):
            qm = only_head(qt, h)
            parts = []
            for c in range(2):
                cols = slice(256 * c, 256 * (c + 1))
                s = nn(kn, qm[:, cols])
                m = jnp.max(s, axis=0, keepdims=True)
                e = jnp.exp2((s - m) * (SCALE * LOG2E))
                inv = 1.0 / jnp.sum(e, axis=0, keepdims=True)
                p = (e * inv).astype(BF)
                probs[w * HEADS + h, :, cols] = p
                parts.append(nn(vt[HD * h : HD * (h + 1)], p))
            mixed.append(jnp.concatenate(parts, axis=1))
        mixed_f = jnp.concatenate(mixed, axis=0)
        mixes[w] = mixed_f
        return carry

    lax.fori_loop(0, 8, attend, 0)

    def mlp(w, carry):
        for part in range(3):

            @pl.when(w == READY[part])
            def _(part=part):
                own_in(up_ref, rg, g_own, part).wait()
                for k in range(3):
                    halo_in(up_ref, rg, g_send, g_recv, part, k).wait_recv()

        lo, hi = offsets(w)
        x = load_window(rx, lo, hi)
        mixed_f = mixes[w]
        mixed = mixed_f.astype(BF)
        branch = nn(wpt[...], mixed).astype(BF)
        y1 = (x + branch.astype(F32)).astype(BF).astype(F32)
        gain_b = wide(gain2[...])
        h2f, n2, r2 = norm_cols(y1, gain_b)
        h2 = h2f.astype(BF)
        u = nn(wet[...], h2)
        u2 = u * u
        t = jnp.tanh(u * (GC + (GC * 0.044715) * u2))
        cdf = 0.5 + 0.5 * t
        act = (u * cdf).astype(BF)
        slope = cdf + (0.5 * u) * (1.0 - t * t) * (GC + (3 * 0.044715 * GC) * u2)
        gf = load_window(rg, lo, hi)
        gb = gf.astype(BF)
        s_red[...] += nt(gb, act)
        du = (nn(wr[...], gb) * slope).astype(BF)
        s_exp[...] += nt(h2, du)
        dh2 = nn(we[...], du)
        s_two[...] += fold(dh2 * n2)
        dy1 = gf + norm_back(dh2, n2, r2, gain_b)
        dy1s[w] = dy1
        da = dy1.astype(BF)
        s_proj[...] += nt(mixed, da)
        dmix = nn(wp[...], da).astype(BF)
        dmixs[w] = dmix
        prod = dmix.astype(F32) * mixed_f
        rows = [jnp.sum(prod[HD * h : HD * (h + 1)], axis=0, keepdims=True) for h in range(HEADS)]
        deltas[w] = jnp.concatenate(rows + [jnp.zeros((8 - HEADS, TOK), F32)], axis=0)
        return carry

    lax.fori_loop(0, 8, mlp, 0)

    two = jnp.broadcast_to(jnp.sum(s_two[...], axis=1, keepdims=True), (D, 32))
    tail = jnp.concatenate([s_proj[...], two], axis=1)
    tiles = [s_red[:, 0:128], s_red[:, 128:256], s_red[:, 256:384]]
    tiles += [s_exp[:, 0:128], s_exp[:, 128:256], s_exp[:, 256:384], tail]
    for j in range(8):
        for i in range(2):
            rows = slice(ROWS_A * i, ROWS_A * (i + 1))
            a_parts[2 * j + i] = tiles[j][rows] if j < 7 else jnp.zeros((ROWS_A, 128), F32)
    reduce_start(a_parts, a_got, a_sems)

    def back(w, carry):
        @pl.when(w > 0)
        def _():
            cols = pl.ds(pl.multiple_of((2 * w - 1) * CH, 128), 2 * CH)
            send_out(ob, out_ref, y_send, y_recv, y_own, cols)

        @pl.when(w == 3)
        def _():
            reduce_middle(a_got, a_cross, a_sems, factor)

        @pl.when(w == 6)
        def _():
            reduce_last(a_cross, a_final, a_sems)

        lo, hi = offsets(w)
        pk = packed[w]
        qt, kt = pk[0:96], pk[96:192]
        vn = vnat[w]
        dmix = dmixs[w]
        delta = deltas[w]
        dqs, dks, dvs = [], [], []
        for h in range(HEADS):
            rows = slice(HD * h, HD * (h + 1))
            dm = only_head(dmix, h)
            dq, dk, dv = [], 0.0, 0.0
            for c in range(2):
                cols = slice(256 * c, 256 * (c + 1))
                p = probs[w * HEADS + h, :, cols]
                dp = nn(vn, dm[:, cols])
                ds = (p.astype(F32) * (dp - delta[h : h + 1, cols]) * SCALE).astype(BF)
                dq.append(nn(kt[rows], ds))
                dk = dk + nt(qt[rows, cols], ds)
                dv = dv + nt(dmix[rows, cols], p)
            dqs.append(jnp.concatenate(dq, axis=1))
            dks.append(dk)
            dvs.append(dv)
        dpk = jnp.concatenate(dqs + dks + dvs, axis=0).astype(BF)
        s_attn[...] += nt(h1s[w], dpk)
        dh1 = nn(wa[...], dpk).astype(BF).astype(F32)
        n1 = n1s[w]
        s_one[...] += fold(dh1 * n1)
        r1 = r1s[w][0:1]
        store_window(ob, lo, hi, dy1s[w] + norm_back(dh1, n1, r1, wide(gain1[...])))
        return carry

    lax.fori_loop(0, 8, back, 0)

    one = jnp.broadcast_to(jnp.sum(s_one[...], axis=1, keepdims=True), (D, 96))
    last = jnp.concatenate([s_attn[:, 256:288], one], axis=1)
    tiles = [s_attn[:, 0:128], s_attn[:, 128:256], last]
    for j in range(4):
        for i in range(4):
            rows = slice(ROWS_B * i, ROWS_B * (i + 1))
            b_parts[4 * j + i] = tiles[j][rows] if j < 3 else jnp.zeros((ROWS_B, 128), F32)
    reduce_start(b_parts, b_got, b_sems)
    for start in (15 * CH, 0):
        send_out(ob, out_ref, y_send, y_recv, y_own, pl.ds(start, CH))
    reduce_middle(b_got, b_cross, b_sems, factor)
    reduce_end(a_final, a_sems)
    fa = [jnp.concatenate([a_final[2 * j], a_final[2 * j + 1]], axis=0) for j in range(7)]
    o_red[...] = jnp.concatenate(fa[0:3], axis=1)
    o_exp[...] = jnp.concatenate(fa[3:6], axis=1)
    o_proj[...] = fa[6][:, 0:96]
    o_two[...] = fa[6].T[96:97]
    reduce_last(b_cross, b_final, b_sems)
    for part in range(3):
        for k in range(3):
            halo_in(tok_ref, rx, x_send, x_recv, part, k).wait_send()
            halo_in(up_ref, rg, g_send, g_recv, part, k).wait_send()
    everything = pl.ds(0, 16 * CH)
    own_out(ob, out_ref, y_own, everything).wait()
    for k in range(3):
        done = halo_out(ob, out_ref, y_send, y_recv, k, everything)
        done.wait_send()
        done.wait_recv()
    reduce_end(b_final, b_sems)
    fb = [jnp.concatenate([b_final[4 * j + i] for i in range(4)], axis=0) for j in range(3)]
    o_attn[...] = jnp.concatenate([fb[0], fb[1], fb[2][:, 0:32]], axis=1)
    o_one[...] = fb[2].T[32:33]


def local(tokens, upstream, gain_one, gain_two, attn_weight, proj_weight, expand_weight, reduce_weight):
    count = tokens.shape[0] * tokens.shape[1] * (tokens.shape[2] // D)
    factor = 1.0 / math.sqrt(count * lax.axis_size("gx") * lax.axis_size("gy"))
    vm = pl.BlockSpec(memory_space=pltpu.VMEM)
    hbm = pl.BlockSpec(memory_space=pl.ANY)
    shape = jax.ShapeDtypeStruct
    dma = pltpu.SemaphoreType.DMA
    outs = pl.pallas_call(
        functools.partial(kernel, factor),
        in_specs=[hbm, hbm] + [vm] * 6,
        out_specs=[hbm] + [vm] * 6,
        out_shape=[
            shape((8, 8, 6144), BF),
            shape((1, D), F32),
            shape((1, D), F32),
            shape((D, 3 * D), F32),
            shape((D, D), F32),
            shape((D, HID), F32),
            shape((D, HID), F32),
        ],
        scratch_shapes=[
            pltpu.VMEM((8, 8, 6144), BF),
            pltpu.VMEM((8, 8, 6144), BF),
            pltpu.VMEM((8, 8, 6144), BF),
            pltpu.VMEM((3 * D, D), BF),
            pltpu.VMEM((D, D), BF),
            pltpu.VMEM((HID, D), BF),
            pltpu.VMEM((HID, D), BF),
            pltpu.VMEM((D, 128), F32),
            pltpu.VMEM((D, 128), F32),
            pltpu.VMEM((D, HID), F32),
            pltpu.VMEM((D, HID), F32),
            pltpu.VMEM((D, D), F32),
            pltpu.VMEM((D, 128), F32),
            pltpu.VMEM((D, 3 * D), F32),
            pltpu.VMEM((D, 128), F32),
            pltpu.VMEM((24, TOK, TOK), BF),
            pltpu.VMEM((8, 3 * D, TOK), BF),
            pltpu.VMEM((8, TOK, D), BF),
            pltpu.VMEM((8, D, TOK), BF),
            pltpu.VMEM((8, D, TOK), F32),
            pltpu.VMEM((8, 8, TOK), F32),
            pltpu.VMEM((8, D, TOK), F32),
            pltpu.VMEM((8, D, TOK), F32),
            pltpu.VMEM((8, D, TOK), BF),
            pltpu.VMEM((8, 8, TOK), F32),
        ]
        + [pltpu.VMEM((GROUP, ROWS_A, 128), F32)] * 4
        + [pltpu.VMEM((GROUP, ROWS_B, 128), F32)] * 4
        + [dma((3, 3))] * 4
        + [dma((3,))] * 2
        + [dma((3,))] * 2
        + [dma, dma((2, 3)), dma((2, 3))],
        compiler_params=pltpu.CompilerParams(
            vmem_limit_bytes=56 * 1024 * 1024, collective_id=0, has_side_effects=True
        ),
        name="block_backward",
    )(
        tokens, upstream, gain_one.reshape(1, D), gain_two.reshape(1, D),
        attn_weight, proj_weight, expand_weight, reduce_weight.T,
    )
    grad, one, two, attn, proj, exp, red = outs
    return (grad, one.reshape(D), two.reshape(D), attn, proj, exp, red.T)


def solution(mesh):
    return jax.shard_map(
        local,
        mesh=mesh,
        in_specs=(P("gx", "gy", None), P("gx", "gy", None), P(), P(), P(), P(), P(), P()),
        out_specs=(P("gx", "gy", None), P(), P(), P(), P(), P(), P()),
        check_vma=False,
    )
```

```python
import functools
import math

import jax
import jax.numpy as jnp
from jax import lax
from jax.experimental import pallas as pl
from jax.experimental.pallas import tpu as pltpu
from jax.sharding import PartitionSpec as P

D = 96
HEADS = 3
HD = 32
WIN = 8
HID = 384
TOK = 512
CH = 384
EPS = 1e-05
F32 = jnp.float32
BF = jnp.bfloat16
SCALE = HD**-0.5
LOG2E = 1.4426950408889634
GC = math.sqrt(2.0 / math.pi)


def nn(a, b):
    return lax.dot_general(a, b, (((1,), (0,)), ((), ())), preferred_element_type=F32)


def nt(a, b):
    return lax.dot_general(a, b, (((1,), (1,)), ((), ())), preferred_element_type=F32)


def wide(col):
    return jnp.concatenate([col] * (TOK // 128), axis=1)


def fold(v):
    return v[:, 0:128] + v[:, 128:256] + v[:, 256:384] + v[:, 384:512]


def mean0(v):
    return jnp.sum(v, axis=0, keepdims=True) * (1.0 / D)


def norm_cols(v, gain):
    c = v - mean0(v)
    r = lax.rsqrt(mean0(c * c) + EPS)
    n = c * r
    return n * gain, n, r


def norm_back(dh, n, r, gain):
    e = dh * gain
    return r * (e - mean0(e) - n * mean0(e * n))


def flip(v):
    return v.astype(F32).T.astype(v.dtype)


def load_window(ref, lo, hi):
    a = ref[:, :, pl.ds(lo, CH)].astype(F32).reshape(64, CH)
    b = ref[:, :, pl.ds(hi, CH)].astype(F32).reshape(64, CH)
    t = jnp.concatenate([a, b], axis=0).T
    return jnp.concatenate([t[0:96], t[96:192], t[192:288], t[288:384]], axis=1)


def store_window(ref, lo, hi, v):
    t = jnp.concatenate([v[:, 128 * i : 128 * (i + 1)] for i in range(4)], axis=0).T
    ref[:, :, pl.ds(lo, CH)] = t[0:64].reshape(8, 8, CH).astype(BF)
    ref[:, :, pl.ds(hi, CH)] = t[64:128].reshape(8, 8, CH).astype(BF)


def only_head(v, h):
    zero = jnp.zeros((HD, v.shape[1]), v.dtype)
    rows = [v[HD * h : HD * (h + 1)] if i == h else zero for i in range(HEADS)]
    return jnp.concatenate(rows, axis=0)


def offsets(w):
    lo = pl.multiple_of((2 * w + 1) * CH, 128)
    hi = pl.multiple_of(lax.rem(2 * w + 2, 16) * CH, 128)
    return lo, hi


MESH = pl.DeviceIdType.MESH
NGX, NGY = 32, 8
GROUP = 16
SHIFTS = ((1, 1), (0, 1), (1, 0))
RELAYS = ((0, 3), (0, 4), (1, 4), (1, -3))
CUTS = (0, 3 * CH, 7 * CH, 13 * CH, 16 * CH)
PARTS = 4
READY = (0, 1, 3, 6)
FORWARD = (0, 1, 2, 3)
ROWS_A, ROWS_B = 48, 16
RELAY_STEP, RELAY_NEXT, RELAY_AT = 3, 4, 3


def half(flag):
    return pl.ds(4, 4) if flag else pl.ds(0, 4)


def place():
    a, b = lax.axis_index("gx"), lax.axis_index("gy")
    first = (b // 4) * 8 + lax.rem(a, 8)
    second = (a // 8) * 4 + lax.rem(b, 4)
    return a, b, first, second


def device(first, second):
    return ((second // 4) * 8 + lax.rem(first, 8), (first // 8) * 4 + lax.rem(second, 4))


def neighbour(dx, dy):
    a, b = lax.axis_index("gx"), lax.axis_index("gy")
    return (lax.rem(a + dx + NGX, NGX), lax.rem(b + dy + NGY, NGY))


def remote(src, dst, send, recv, where):
    return pltpu.make_async_remote_copy(
        src_ref=src, dst_ref=dst, send_sem=send, recv_sem=recv, device_id=where, device_id_type=MESH
    )


def halo_in(src, dst, send, recv, part, k):
    dx, dy = SHIFTS[k]
    cols = pl.ds(CUTS[part], CUTS[part + 1] - CUTS[part])
    return remote(
        src.at[half(not dx), half(not dy), cols], dst.at[half(dx), half(dy), cols],
        send.at[part, k], recv.at[part, k], neighbour(-dx, -dy),
    )


def relay_in(src, dst, send, recv, part, k):
    dx, dy = SHIFTS[k]
    cols = pl.ds(CUTS[part], CUTS[part + 1] - CUTS[part])
    a, b = neighbour(-dx, RELAY_STEP)
    return remote(
        src.at[half(not dx), half(not dy), cols], dst.at[half(dx), half(dy), cols],
        send.at[part, k], recv.at[part, k], (a, b),
    )


def relay_on(src, dst, send, recv, part, k):
    dx, dy = SHIFTS[k]
    cols = pl.ds(CUTS[part], CUTS[part + 1] - CUTS[part])
    box = (half(dx), half(dy), cols)
    return remote(
        src.at[box], dst.at[box], send.at[part, k], recv.at[part, k], neighbour(0, RELAY_NEXT)
    )


def own_in(src, dst, sem, part):
    cols = pl.ds(CUTS[part], CUTS[part + 1] - CUTS[part])
    return pltpu.make_async_copy(
        src.at[half(1), half(1), cols], dst.at[half(0), half(0), cols], sem.at[part]
    )


def halo_out(src, dst, send, recv, k, cols):
    dx, dy = SHIFTS[k]
    return remote(
        src.at[half(dx), half(dy), cols], dst.at[half(not dx), half(not dy), cols],
        send.at[k], recv.at[k], neighbour(dx, dy),
    )


def own_out(src, dst, sem, cols):
    return pltpu.make_async_copy(
        src.at[half(0), half(0), cols], dst.at[half(1), half(1), cols], sem
    )


def send_out(src, dst, send, recv, sem, cols):
    for k in range(3):
        halo_out(src, dst, send, recv, k, cols).start()
    own_out(src, dst, sem, cols).start()


def spread(src_of, dst, slot, send, recv, along_first):
    a, b, first, second = place()
    mine = first if along_first else second

    def step(r, carry):
        to = lax.rem(mine + r, GROUP)
        where = device(to, second) if along_first else device(first, to)
        remote(src_of(to), dst.at[slot], send, recv, where).start()
        return carry

    lax.fori_loop(1, GROUP, step, 0)


def settle(buf, send, recv):
    most = buf.at[pl.ds(0, GROUP - 1)]
    done = remote(most, most, send, recv, neighbour(1, 0))
    done.wait_recv()
    done.wait_send()


def total(buf):
    acc = buf[0]
    for i in range(1, GROUP):
        acc = acc + buf[i]
    return acc


def reduce_start(parts, got, sems):
    a, b, first, second = place()
    got[first] = parts[first]
    spread(lambda to: parts.at[to], got, first, sems.at[0, 0], sems.at[1, 0], True)


def reduce_middle(got, cross, sems, factor):
    a, b, first, second = place()
    settle(got, sems.at[0, 0], sems.at[1, 0])
    cross[second] = total(got) * factor
    spread(lambda to: cross.at[second], cross, second, sems.at[0, 1], sems.at[1, 1], False)


def reduce_last(cross, final, sems):
    a, b, first, second = place()
    settle(cross, sems.at[0, 1], sems.at[1, 1])
    final[first] = total(cross)
    spread(lambda to: final.at[first], final, first, sems.at[0, 2], sems.at[1, 2], True)


def reduce_end(final, sems):
    settle(final, sems.at[0, 2], sems.at[1, 2])


def attn_forward(w, qt, kn, vt, probs, sbuf):
    units = [(h, c) for h in range(HEADS) for c in range(2)]
    top, mixed = {}, {}
    sums = {}

    def rows_of(j):
        return slice(64 * j, 64 * (j + 1))

    def score(t, j):
        h, c = units[t]
        s = nn(kn[rows_of(j)], heads[h][:, 256 * c : 256 * (c + 1)])
        sbuf[t % 3, rows_of(j), :] = s
        m = jnp.max(s.reshape(64 // 8, 8, 256), axis=0)
        top[t] = m if j == 0 else jnp.maximum(top[t], m)

    def power(t, j, m):
        e = jnp.exp2((sbuf[t % 3, rows_of(j), :] - m) * (SCALE * LOG2E))
        sbuf[t % 3, rows_of(j), :] = e
        part = jnp.sum(e.reshape(64 // 8, 8, 256), axis=0)
        sums[t] = part if j == 0 else sums[t] + part

    def weigh(t, j, inv):
        h, c = units[t]
        p = (sbuf[t % 3, rows_of(j), :] * inv).astype(BF)
        probs[w * HEADS + h, rows_of(j), 256 * c : 256 * (c + 1)] = p

    def mix(t):
        h, c = units[t]
        p = probs[w * HEADS + h, :, 256 * c : 256 * (c + 1)]
        mixed[t] = nn(vt[HD * h : HD * (h + 1)], p)

    heads = [only_head(qt, h) for h in range(HEADS)]
    n, steps = len(units), TOK // 64
    for t in range(-1, n + 1):
        if 0 <= t < n:
            m = jnp.max(top[t], axis=0, keepdims=True)
        if t >= 1:
            inv = 1.0 / jnp.sum(sums[t - 1], axis=0, keepdims=True)
        for j in range(steps):
            if t + 1 < n:
                score(t + 1, j)
            if 0 <= t < n:
                power(t, j, m)
            if t >= 1:
                weigh(t - 1, j, inv)
        if t >= 1:
            mix(t - 1)
    out = [jnp.concatenate([mixed[2 * h], mixed[2 * h + 1]], axis=1) for h in range(HEADS)]
    return jnp.concatenate(out, axis=0)


def attn_backward(w, qt, kt, vn, dmix, delta, probs, dbuf, ebuf):
    units = [(h, k, c) for h in range(HEADS) for c in range(2) for k in range(2)]
    dq, dk, dv = {}, {}, {}
    heads = [only_head(dmix, h) for h in range(HEADS)]

    def tile(i):
        return slice(256 * i, 256 * (i + 1))

    def grow(table, key, v):
        table[key] = v if key not in table else table[key] + v

    def first(t, j):
        h, k, c = units[t]
        rows = slice(256 * k + 128 * j, 256 * k + 128 * (j + 1))
        dbuf[t % 2, 128 * j : 128 * (j + 1), :] = nn(vn[rows], heads[h][:, tile(c)])

    def middle(t, j):
        h, k, c = units[t]
        rows = slice(256 * k + 128 * j, 256 * k + 128 * (j + 1))
        p = probs[w * HEADS + h, rows, tile(c)].astype(F32)
        dp = dbuf[t % 2, 128 * j : 128 * (j + 1), :]
        ds = p * (dp - delta[h : h + 1, tile(c)]) * SCALE
        ebuf[t % 2, 128 * j : 128 * (j + 1), :] = ds.astype(BF)

    def last(t, j):
        h, k, c = units[t]
        rows = slice(HD * h, HD * (h + 1))
        ds = ebuf[t % 2]
        if j == 0:
            grow(dq, (h, c), nn(kt[rows, tile(k)], ds))
        elif j == 1:
            grow(dk, (h, k), nt(qt[rows, tile(c)], ds))
        elif j == 2:
            grow(dv, (h, k), nt(dmix[rows, tile(c)], probs[w * HEADS + h, tile(k), tile(c)]))

    n = len(units)
    for t in range(-1, n + 1):
        for j in range(max(256 // 128, 3)):
            if t + 1 < n and j < 256 // 128:
                first(t + 1, j)
            if t >= 1:
                last(t - 1, j)
            if 0 <= t < n and j < 256 // 128:
                middle(t, j)
    parts = [jnp.concatenate([v[h, 0], v[h, 1]], axis=1) for v in (dq, dk, dv) for h in range(HEADS)]
    return jnp.concatenate(parts, axis=0).astype(BF)


def mlp_middle(h2, gb, wet, wr, acts, dus, ubuf):
    blocks = [(r, c) for c in range(TOK // 256) for r in range(HID // 64)]

    def box(t):
        r, c = blocks[t]
        return slice(64 * r, 64 * (r + 1)), slice(256 * c, 256 * (c + 1))

    def first(t):
        rows, cols = box(t)
        ubuf[t % 2, 0] = nn(wet[rows, :], h2[:, cols])
        ubuf[t % 2, 1] = nn(wr[rows, :], gb[:, cols])

    def second(t):
        rows, cols = box(t)
        u = ubuf[t % 2, 0]
        u2 = u * u
        v = u * (GC + (GC * 0.044715) * u2)
        th = jnp.tanh(v)
        cdf = 0.5 + 0.5 * th
        acts[rows, cols] = (u * cdf).astype(BF)
        slope = cdf + (0.5 - 0.5 * (th * th)) * (u * (GC + (3 * 0.044715 * GC) * u2))
        dus[rows, cols] = (ubuf[t % 2, 1] * slope).astype(BF)

    for t in range(-1, len(blocks)):
        if t + 1 < len(blocks):
            first(t + 1)
        if t >= 0:
            second(t)


def kernel(
    factor, tok_ref, up_ref, gain1_ref, gain2_ref, wa, wp, we, wrt,
    out_ref, o_one, o_two, o_attn, o_proj, o_exp, o_red,
    rx, rg, rb, ob, wat, wpt, wet, wr, gain1, gain2,
    s_red, s_exp, s_proj, s_two, s_attn, s_one,
    probs, packed, vnat, h1s, n1s, r1s, mixes, dy1s, dmixs, deltas, sbuf, dbuf, ebuf, acts, dus, ubuf,
    a_parts, a_got, a_cross, a_final, b_parts, b_got, b_cross, b_final,
    x_send, x_recv, g_send, g_recv, x_own, g_own, y_send, y_recv, y_own, z_send, z_recv, a_sems, b_sems,
):
    a, b, first, second = place()
    barrier = pltpu.get_barrier_semaphore()
    for dx, dy in SHIFTS:
        for sign in (-1, 1):
            pl.semaphore_signal(
                barrier, inc=1, device_id=neighbour(sign * dx, sign * dy), device_id_type=MESH
            )

    for dx, dy in RELAYS:
        for sign in (-1, 1):
            pl.semaphore_signal(
                barrier, inc=1, device_id=neighbour(sign * dx, sign * dy), device_id_type=MESH
            )

    def greet(r, carry):
        pl.semaphore_signal(
            barrier, inc=1, device_id=device(lax.rem(first + r, GROUP), second), device_id_type=MESH
        )
        pl.semaphore_signal(
            barrier, inc=1, device_id=device(first, lax.rem(second + r, GROUP)), device_id_type=MESH
        )
        return carry

    lax.fori_loop(1, GROUP, greet, 0)
    for part in range(PARTS):
        own_in(tok_ref, rx, x_own, part).start()
        own_in(up_ref, rg, g_own, part).start()
    pl.semaphore_wait(barrier, 2 * len(SHIFTS) + 2 * len(RELAYS) + 2 * (GROUP - 1))
    for part in range(PARTS):
        for k in range(3):
            halo_in(tok_ref, rx, x_send, x_recv, part, k).start()
    edge = lax.rem(b, 4) == 0
    relay = lax.rem(b, 4) == RELAY_AT
    for part in range(PARTS):
        halo_in(up_ref, rg, g_send, g_recv, part, 2).start()

    @pl.when(jnp.logical_not(edge))
    def _():
        for part in range(PARTS):
            for k in range(2):
                halo_in(up_ref, rg, g_send, g_recv, part, k).start()

    @pl.when(edge)
    def _():
        for part in range(PARTS):
            for k in range(2):
                relay_in(up_ref, rb, g_send, z_recv, part, k).start()

    def forward(part):
        @pl.when(relay)
        def _():
            for k in range(2):
                relay_in(up_ref, rb, g_send, z_recv, part, k).wait_recv()
                relay_on(rb, rg, z_send, g_recv, part, k).start()

    wat[...] = flip(wa[...])
    wpt[...] = flip(wp[...])
    wet[...] = flip(we[...])
    wr[...] = flip(wrt[...])
    gain1[...] = jnp.broadcast_to(gain1_ref[...], (128, D)).T
    gain2[...] = jnp.broadcast_to(gain2_ref[...], (128, D)).T
    s_red[...] = jnp.zeros_like(s_red)
    s_exp[...] = jnp.zeros_like(s_exp)
    s_proj[...] = jnp.zeros_like(s_proj)
    s_two[...] = jnp.zeros_like(s_two)
    s_attn[...] = jnp.zeros_like(s_attn)
    s_one[...] = jnp.zeros_like(s_one)

    def attend(w, carry):
        for part in range(PARTS):

            @pl.when(w == FORWARD[part])
            def _(part=part):
                forward(part)

        for part in range(PARTS):

            @pl.when(w == READY[part])
            def _(part=part):
                own_in(tok_ref, rx, x_own, part).wait()
                for k in range(3):
                    halo_in(tok_ref, rx, x_send, x_recv, part, k).wait_recv()

        lo, hi = offsets(w)
        x = load_window(rx, lo, hi)
        h1f, n1, r1 = norm_cols(x, wide(gain1[...]))
        h1 = h1f.astype(BF)
        h1s[w] = h1
        n1s[w] = n1
        r1s[w] = jnp.broadcast_to(r1, (8, TOK))
        pk = nn(wat[...], h1).astype(BF)
        packed[w] = pk
        qt, vt = pk[0:96], pk[192:288]
        kn = pk[96:192].T
        vnat[w] = vt.T
        mixed_f = attn_forward(w, qt, kn, vt, probs, sbuf)
        mixes[w] = mixed_f
        return carry

    lax.fori_loop(0, 8, attend, 0)

    def mlp(w, carry):
        for part in range(PARTS):

            @pl.when(w == READY[part])
            def _(part=part):
                own_in(up_ref, rg, g_own, part).wait()
                for k in range(3):
                    halo_in(up_ref, rg, g_send, g_recv, part, k).wait_recv()

        lo, hi = offsets(w)
        x = load_window(rx, lo, hi)
        mixed_f = mixes[w]
        mixed = mixed_f.astype(BF)
        branch = nn(wpt[...], mixed).astype(BF)
        y1 = (x + branch.astype(F32)).astype(BF).astype(F32)
        gain_b = wide(gain2[...])
        h2f, n2, r2 = norm_cols(y1, gain_b)
        h2 = h2f.astype(BF)
        gf = load_window(rg, lo, hi)
        gb = gf.astype(BF)
        mlp_middle(h2, gb, wet, wr, acts, dus, ubuf)
        s_red[...] += nt(gb, acts[...])
        du = dus[...]
        s_exp[...] += nt(h2, du)
        dh2 = nn(we[...], du)
        s_two[...] += fold(dh2 * n2)
        dy1 = gf + norm_back(dh2, n2, r2, gain_b)
        dy1s[w] = dy1
        da = dy1.astype(BF)
        s_proj[...] += nt(mixed, da)
        dmix = nn(wp[...], da).astype(BF)
        dmixs[w] = dmix
        prod = dmix.astype(F32) * mixed_f
        rows = [jnp.sum(prod[HD * h : HD * (h + 1)], axis=0, keepdims=True) for h in range(HEADS)]
        deltas[w] = jnp.concatenate(rows + [jnp.zeros((8 - HEADS, TOK), F32)], axis=0)
        return carry

    lax.fori_loop(0, 8, mlp, 0)

    two = jnp.broadcast_to(jnp.sum(s_two[...], axis=1, keepdims=True), (D, 32))
    tail = jnp.concatenate([s_proj[...], two], axis=1)
    tiles = [s_red[:, 0:128], s_red[:, 128:256], s_red[:, 256:384]]
    tiles += [s_exp[:, 0:128], s_exp[:, 128:256], s_exp[:, 256:384], tail]
    for j in range(8):
        for i in range(2):
            rows = slice(ROWS_A * i, ROWS_A * (i + 1))
            a_parts[2 * j + i] = tiles[j][rows] if j < 7 else jnp.zeros((ROWS_A, 128), F32)
    reduce_start(a_parts, a_got, a_sems)

    def back(w, carry):
        @pl.when(w > 0)
        def _():
            cols = pl.ds(pl.multiple_of((2 * w - 1) * CH, 128), 2 * CH)
            send_out(ob, out_ref, y_send, y_recv, y_own, cols)

        @pl.when(w == 3)
        def _():
            reduce_middle(a_got, a_cross, a_sems, factor)

        @pl.when(w == 6)
        def _():
            reduce_last(a_cross, a_final, a_sems)

        lo, hi = offsets(w)
        pk = packed[w]
        qt, kt = pk[0:96], pk[96:192]
        vn = vnat[w]
        dmix = dmixs[w]
        delta = deltas[w]
        dpk = attn_backward(w, qt, kt, vn, dmix, delta, probs, dbuf, ebuf)
        s_attn[...] += nt(h1s[w], dpk)
        dh1 = nn(wa[...], dpk).astype(BF).astype(F32)
        n1 = n1s[w]
        s_one[...] += fold(dh1 * n1)
        r1 = r1s[w][0:1]
        store_window(ob, lo, hi, dy1s[w] + norm_back(dh1, n1, r1, wide(gain1[...])))
        return carry

    lax.fori_loop(0, 8, back, 0)

    for j in range(2):
        for i in range(6):
            b_parts[6 * j + i] = s_attn[16 * i : 16 * i + 16, 128 * j : 128 * j + 128]
    rest = s_attn[:, 256:288]
    rest = jnp.concatenate([rest[24 * i : 24 * i + 24] for i in range(4)], axis=1)
    one = jnp.broadcast_to(jnp.sum(s_one[...], axis=1, keepdims=True), (D, 128)).T[0:8]
    rest = jnp.concatenate([rest, jnp.concatenate([one, jnp.zeros((8, 32), F32)], axis=1)], axis=0)
    b_parts[12] = rest[0:16]
    b_parts[13] = rest[16:32]
    for i in range(14, GROUP):
        b_parts[i] = jnp.zeros((ROWS_B, 128), F32)
    reduce_start(b_parts, b_got, b_sems)
    for start in (15 * CH, 0):
        send_out(ob, out_ref, y_send, y_recv, y_own, pl.ds(start, CH))
    reduce_middle(b_got, b_cross, b_sems, factor)
    reduce_end(a_final, a_sems)
    fa = [jnp.concatenate([a_final[2 * j], a_final[2 * j + 1]], axis=0) for j in range(7)]
    o_red[...] = jnp.concatenate(fa[0:3], axis=1)
    o_exp[...] = jnp.concatenate(fa[3:6], axis=1)
    o_proj[...] = fa[6][:, 0:96]
    o_two[...] = fa[6].T[96:97]
    reduce_last(b_cross, b_final, b_sems)
    for part in range(PARTS):
        for k in range(3):
            halo_in(tok_ref, rx, x_send, x_recv, part, k).wait_send()
            halo_in(up_ref, rg, g_send, g_recv, part, k).wait_send()

    @pl.when(relay)
    def _():
        for part in range(PARTS):
            for k in range(2):
                relay_on(rb, rg, z_send, g_recv, part, k).wait_send()

    everything = pl.ds(0, 16 * CH)
    own_out(ob, out_ref, y_own, everything).wait()
    for k in range(3):
        done = halo_out(ob, out_ref, y_send, y_recv, k, everything)
        done.wait_send()
        done.wait_recv()
    reduce_end(b_final, b_sems)
    fb = [jnp.concatenate([b_final[6 * j + i] for i in range(6)], axis=0) for j in range(2)]
    rest = jnp.concatenate([b_final[12], b_final[13]], axis=0)
    last = jnp.concatenate([rest[0:24, 32 * i : 32 * i + 32] for i in range(4)], axis=0)
    o_attn[...] = jnp.concatenate(fb + [last], axis=1)
    o_one[...] = rest[24:25, 0:96]


def local(tokens, upstream, gain_one, gain_two, attn_weight, proj_weight, expand_weight, reduce_weight):
    count = tokens.shape[0] * tokens.shape[1] * (tokens.shape[2] // D)
    factor = 1.0 / math.sqrt(count * lax.axis_size("gx") * lax.axis_size("gy"))
    vm = pl.BlockSpec(memory_space=pltpu.VMEM)
    hbm = pl.BlockSpec(memory_space=pl.ANY)
    shape = jax.ShapeDtypeStruct
    dma = pltpu.SemaphoreType.DMA
    outs = pl.pallas_call(
        functools.partial(kernel, factor),
        in_specs=[hbm, hbm] + [vm] * 6,
        out_specs=[hbm] + [vm] * 6,
        out_shape=[
            shape((8, 8, 6144), BF),
            shape((1, D), F32),
            shape((1, D), F32),
            shape((D, 3 * D), F32),
            shape((D, D), F32),
            shape((D, HID), F32),
            shape((D, HID), F32),
        ],
        scratch_shapes=[
            pltpu.VMEM((8, 8, 6144), BF),
            pltpu.VMEM((8, 8, 6144), BF),
            pltpu.VMEM((8, 8, 6144), BF),
            pltpu.VMEM((8, 8, 6144), BF),
            pltpu.VMEM((3 * D, D), BF),
            pltpu.VMEM((D, D), BF),
            pltpu.VMEM((HID, D), BF),
            pltpu.VMEM((HID, D), BF),
            pltpu.VMEM((D, 128), F32),
            pltpu.VMEM((D, 128), F32),
            pltpu.VMEM((D, HID), F32),
            pltpu.VMEM((D, HID), F32),
            pltpu.VMEM((D, D), F32),
            pltpu.VMEM((D, 128), F32),
            pltpu.VMEM((D, 3 * D), F32),
            pltpu.VMEM((D, 128), F32),
            pltpu.VMEM((24, TOK, TOK), BF),
            pltpu.VMEM((8, 3 * D, TOK), BF),
            pltpu.VMEM((8, TOK, D), BF),
            pltpu.VMEM((8, D, TOK), BF),
            pltpu.VMEM((8, D, TOK), F32),
            pltpu.VMEM((8, 8, TOK), F32),
            pltpu.VMEM((8, D, TOK), F32),
            pltpu.VMEM((8, D, TOK), F32),
            pltpu.VMEM((8, D, TOK), BF),
            pltpu.VMEM((8, 8, TOK), F32),
            pltpu.VMEM((3, TOK, 256), F32),
            pltpu.VMEM((2, 256, 256), F32),
            pltpu.VMEM((2, 256, 256), BF),
            pltpu.VMEM((HID, TOK), BF),
            pltpu.VMEM((HID, TOK), BF),
            pltpu.VMEM((2, 2, 64, 256), F32),
        ]
        + [pltpu.VMEM((GROUP, ROWS_A, 128), F32)] * 4
        + [pltpu.VMEM((GROUP, ROWS_B, 128), F32)] * 4
        + [dma((PARTS, 3))] * 4
        + [dma((PARTS,))] * 2
        + [dma((3,))] * 2
        + [dma, dma((PARTS, 3)), dma((PARTS, 3)), dma((2, 3)), dma((2, 3))],
        compiler_params=pltpu.CompilerParams(
            vmem_limit_bytes=56 * 1024 * 1024, collective_id=0, has_side_effects=True
        ),
        name="block_backward",
    )(
        tokens, upstream, gain_one.reshape(1, D), gain_two.reshape(1, D),
        attn_weight, proj_weight, expand_weight, reduce_weight.T,
    )
    grad, one, two, attn, proj, exp, red = outs
    return (grad, one.reshape(D), two.reshape(D), attn, proj, exp, red.T)


def solution(mesh):
    return jax.shard_map(
        local,
        mesh=mesh,
        in_specs=(P("gx", "gy", None), P("gx", "gy", None), P(), P(), P(), P(), P(), P()),
        out_specs=(P("gx", "gy", None), P(), P(), P(), P(), P(), P()),
        check_vma=False,
    )
```

```python
import functools
import math

import jax
import jax.numpy as jnp
from jax import lax
from jax.experimental import pallas as pl
from jax.experimental.pallas import tpu as pltpu
from jax.sharding import PartitionSpec as P

D = 96
HEADS = 3
HD = 32
WIN = 8
HID = 384
TOK = 512
CH = 384
EPS = 1e-05
F32 = jnp.float32
BF = jnp.bfloat16
SCALE = HD**-0.5
LOG2E = 1.4426950408889634
GC = math.sqrt(2.0 / math.pi)


def nn(a, b):
    return lax.dot_general(a, b, (((1,), (0,)), ((), ())), preferred_element_type=F32)


def nt(a, b):
    return lax.dot_general(a, b, (((1,), (1,)), ((), ())), preferred_element_type=F32)


def wide(col):
    return jnp.concatenate([col] * (TOK // 128), axis=1)


def fold(v):
    return v[:, 0:128] + v[:, 128:256] + v[:, 256:384] + v[:, 384:512]


def mean0(v):
    return jnp.sum(v, axis=0, keepdims=True) * (1.0 / D)


def norm_cols(v, gain):
    c = v - mean0(v)
    r = lax.rsqrt(mean0(c * c) + EPS)
    n = c * r
    return n * gain, n, r


def norm_back(dh, n, r, gain):
    e = dh * gain
    return r * (e - mean0(e) - n * mean0(e * n))


def flip(v):
    return v.astype(F32).T.astype(v.dtype)


def load_window(ref, lo, hi):
    a = ref[:, :, pl.ds(lo, CH)].astype(F32).reshape(64, CH)
    b = ref[:, :, pl.ds(hi, CH)].astype(F32).reshape(64, CH)
    t = jnp.concatenate([a, b], axis=0).T
    return jnp.concatenate([t[0:96], t[96:192], t[192:288], t[288:384]], axis=1)


def store_window(ref, lo, hi, v):
    t = jnp.concatenate([v[:, 128 * i : 128 * (i + 1)] for i in range(4)], axis=0).T
    ref[:, :, pl.ds(lo, CH)] = t[0:64].reshape(8, 8, CH).astype(BF)
    ref[:, :, pl.ds(hi, CH)] = t[64:128].reshape(8, 8, CH).astype(BF)


def only_head(v, h):
    zero = jnp.zeros((HD, v.shape[1]), v.dtype)
    rows = [v[HD * h : HD * (h + 1)] if i == h else zero for i in range(HEADS)]
    return jnp.concatenate(rows, axis=0)


def offsets(w):
    lo = pl.multiple_of((2 * w + 1) * CH, 128)
    hi = pl.multiple_of(lax.rem(2 * w + 2, 16) * CH, 128)
    return lo, hi


MESH = pl.DeviceIdType.MESH
NGX, NGY = 32, 8
GROUP = 16
SHIFTS = ((1, 1), (0, 1), (1, 0))
RELAYS = ((1, -3), (0, 4))
CUTS = (0, 3 * CH, 7 * CH, 13 * CH, 16 * CH)
PARTS = 4
READY = (0, 1, 3, 6)
FORWARD = (
    (0, 0, True), (1, 1, True), (2, 2, True), (3, 3, True),
    (3, 0, False), (4, 1, False), (5, 2, False), (6, 3, False),
)
ROWS_A, ROWS_B = 48, 16


def half(flag):
    return pl.ds(4, 4) if flag else pl.ds(0, 4)


def place():
    a, b = lax.axis_index("gx"), lax.axis_index("gy")
    first = (b // 4) * 8 + lax.rem(a, 8)
    second = (a // 8) * 4 + lax.rem(b, 4)
    return a, b, first, second


def device(first, second):
    return ((second // 4) * 8 + lax.rem(first, 8), (first // 8) * 4 + lax.rem(second, 4))


def neighbour(dx, dy):
    a, b = lax.axis_index("gx"), lax.axis_index("gy")
    return (lax.rem(a + dx + NGX, NGX), lax.rem(b + dy + NGY, NGY))


def remote(src, dst, send, recv, where):
    return pltpu.make_async_remote_copy(
        src_ref=src, dst_ref=dst, send_sem=send, recv_sem=recv, device_id=where, device_id_type=MESH
    )


def halo_in(src, dst, send, recv, part, k):
    dx, dy = SHIFTS[k]
    cols = pl.ds(CUTS[part], CUTS[part + 1] - CUTS[part])
    return remote(
        src.at[half(not dx), half(not dy), cols], dst.at[half(dx), half(dy), cols],
        send.at[part, k], recv.at[part, k], neighbour(-dx, -dy),
    )


def relay_in(src, dst, send, recv, part):
    cols = pl.ds(CUTS[part], CUTS[part + 1] - CUTS[part])
    return remote(
        src.at[half(0), half(0), cols], dst.at[half(1), half(1), cols],
        send.at[part, 0], recv.at[part], neighbour(-1, 3),
    )


def relay_on(src, dst, send, recv, part):
    box = (half(1), half(1), pl.ds(CUTS[part], CUTS[part + 1] - CUTS[part]))
    return remote(src.at[box], dst.at[box], send.at[part], recv.at[part, 0], neighbour(0, 4))


def piece(i):
    if i < 7:
        return pl.ds((2 * i + 1) * CH, 2 * CH)
    return pl.ds(15 * CH if i == 7 else 0, CH)


def relay_out(src, dst, send, recv, cols, i):
    box = (half(1), half(1), cols)
    return remote(src.at[box], dst.at[box], send.at[0], recv.at[i], neighbour(1, -3))


def relay_done(src, dst, send, recv, cols):
    return remote(
        src.at[half(1), half(1), cols], dst.at[half(0), half(0), cols],
        send, recv.at[0], neighbour(0, 4),
    )


def own_in(src, dst, sem, part):
    cols = pl.ds(CUTS[part], CUTS[part + 1] - CUTS[part])
    return pltpu.make_async_copy(
        src.at[half(1), half(1), cols], dst.at[half(0), half(0), cols], sem.at[part]
    )


def halo_out(src, dst, send, recv, k, cols):
    dx, dy = SHIFTS[k]
    return remote(
        src.at[half(dx), half(dy), cols], dst.at[half(not dx), half(not dy), cols],
        send.at[k], recv.at[k], neighbour(dx, dy),
    )


def own_out(src, dst, sem, cols):
    return pltpu.make_async_copy(
        src.at[half(0), half(0), cols], dst.at[half(1), half(1), cols], sem
    )


def send_out(src, dst, send, recv, sem, via, via_recv, cols, i):
    edge = lax.rem(lax.axis_index("gy"), 4) == 3

    @pl.when(edge)
    def _():
        relay_out(src, via, send, via_recv, cols, i).start()

    @pl.when(jnp.logical_not(edge))
    def _():
        halo_out(src, dst, send, recv, 0, cols).start()

    for k in (1, 2):
        halo_out(src, dst, send, recv, k, cols).start()
    own_out(src, dst, sem, cols).start()


def spread(src_of, dst, slot, send, recv, along_first):
    a, b, first, second = place()
    mine = first if along_first else second

    def step(r, carry):
        to = lax.rem(mine + r, GROUP)
        where = device(to, second) if along_first else device(first, to)
        remote(src_of(to), dst.at[slot], send, recv, where).start()
        return carry

    lax.fori_loop(1, GROUP, step, 0)


def settle(buf, send, recv):
    most = buf.at[pl.ds(0, GROUP - 1)]
    done = remote(most, most, send, recv, neighbour(1, 0))
    done.wait_recv()
    done.wait_send()


def total(buf):
    acc = buf[0]
    for i in range(1, GROUP):
        acc = acc + buf[i]
    return acc


def reduce_start(parts, got, sems):
    a, b, first, second = place()
    got[first] = parts[first]
    spread(lambda to: parts.at[to], got, first, sems.at[0, 0], sems.at[1, 0], True)


def reduce_middle(got, cross, sems, factor):
    a, b, first, second = place()
    settle(got, sems.at[0, 0], sems.at[1, 0])
    cross[second] = total(got) * factor
    spread(lambda to: cross.at[second], cross, second, sems.at[0, 1], sems.at[1, 1], False)


def reduce_last(cross, final, sems):
    a, b, first, second = place()
    settle(cross, sems.at[0, 1], sems.at[1, 1])
    final[first] = total(cross)
    spread(lambda to: final.at[first], final, first, sems.at[0, 2], sems.at[1, 2], True)


def reduce_end(final, sems):
    settle(final, sems.at[0, 2], sems.at[1, 2])


def attn_forward(w, qt, kn, vt, probs, sbuf):
    units = [(h, c) for h in range(HEADS) for c in range(2)]
    top, mixed = {}, {}
    sums = {}

    def rows_of(j):
        return slice(64 * j, 64 * (j + 1))

    def score(t, j):
        h, c = units[t]
        s = nn(kn[rows_of(j)], heads[h][:, 256 * c : 256 * (c + 1)])
        sbuf[t % 3, rows_of(j), :] = s
        m = jnp.max(s.reshape(64 // 8, 8, 256), axis=0)
        top[t] = m if j == 0 else jnp.maximum(top[t], m)

    def power(t, j, m):
        e = jnp.exp2((sbuf[t % 3, rows_of(j), :] - m) * (SCALE * LOG2E))
        sbuf[t % 3, rows_of(j), :] = e
        part = jnp.sum(e.reshape(64 // 8, 8, 256), axis=0)
        sums[t] = part if j == 0 else sums[t] + part

    def weigh(t, j, inv):
        h, c = units[t]
        p = (sbuf[t % 3, rows_of(j), :] * inv).astype(BF)
        probs[w * HEADS + h, rows_of(j), 256 * c : 256 * (c + 1)] = p

    def mix(t):
        h, c = units[t]
        p = probs[w * HEADS + h, :, 256 * c : 256 * (c + 1)]
        mixed[t] = nn(vt[HD * h : HD * (h + 1)], p)

    heads = [only_head(qt, h) for h in range(HEADS)]
    n, steps = len(units), TOK // 64
    for t in range(-1, n + 1):
        if 0 <= t < n:
            m = jnp.max(top[t], axis=0, keepdims=True)
        if t >= 1:
            inv = 1.0 / jnp.sum(sums[t - 1], axis=0, keepdims=True)
        for j in range(steps):
            if t + 1 < n:
                score(t + 1, j)
            if 0 <= t < n:
                power(t, j, m)
            if t >= 1:
                weigh(t - 1, j, inv)
        if t >= 1:
            mix(t - 1)
    out = [jnp.concatenate([mixed[2 * h], mixed[2 * h + 1]], axis=1) for h in range(HEADS)]
    return jnp.concatenate(out, axis=0)


def attn_backward(w, qt, kt, vn, dmix, delta, probs, dbuf, ebuf):
    units = [(h, k, c) for h in range(HEADS) for c in range(2) for k in range(2)]
    dq, dk, dv = {}, {}, {}
    heads = [only_head(dmix, h) for h in range(HEADS)]

    def tile(i):
        return slice(256 * i, 256 * (i + 1))

    def grow(table, key, v):
        table[key] = v if key not in table else table[key] + v

    def first(t, j):
        h, k, c = units[t]
        rows = slice(256 * k + 128 * j, 256 * k + 128 * (j + 1))
        dbuf[t % 2, 128 * j : 128 * (j + 1), :] = nn(vn[rows], heads[h][:, tile(c)])

    def middle(t, j):
        h, k, c = units[t]
        rows = slice(256 * k + 128 * j, 256 * k + 128 * (j + 1))
        p = probs[w * HEADS + h, rows, tile(c)].astype(F32)
        dp = dbuf[t % 2, 128 * j : 128 * (j + 1), :]
        ds = p * (dp - delta[h : h + 1, tile(c)]) * SCALE
        ebuf[t % 2, 128 * j : 128 * (j + 1), :] = ds.astype(BF)

    def last(t, j):
        h, k, c = units[t]
        rows = slice(HD * h, HD * (h + 1))
        ds = ebuf[t % 2]
        if j == 0:
            grow(dq, (h, c), nn(kt[rows, tile(k)], ds))
        elif j == 1:
            grow(dk, (h, k), nt(qt[rows, tile(c)], ds))
        elif j == 2:
            grow(dv, (h, k), nt(dmix[rows, tile(c)], probs[w * HEADS + h, tile(k), tile(c)]))

    n = len(units)
    for t in range(-1, n + 1):
        for j in range(max(256 // 128, 3)):
            if t + 1 < n and j < 256 // 128:
                first(t + 1, j)
            if t >= 1:
                last(t - 1, j)
            if 0 <= t < n and j < 256 // 128:
                middle(t, j)
    parts = [jnp.concatenate([v[h, 0], v[h, 1]], axis=1) for v in (dq, dk, dv) for h in range(HEADS)]
    return jnp.concatenate(parts, axis=0).astype(BF)


def mlp_middle(h2, gb, wet, wr, acts, dus, ubuf):
    blocks = [(r, c) for c in range(TOK // 256) for r in range(HID // 64)]

    def box(t):
        r, c = blocks[t]
        return slice(64 * r, 64 * (r + 1)), slice(256 * c, 256 * (c + 1))

    def first(t):
        rows, cols = box(t)
        ubuf[t % 2, 0] = nn(wet[rows, :], h2[:, cols])
        ubuf[t % 2, 1] = nn(wr[rows, :], gb[:, cols])

    def second(t):
        rows, cols = box(t)
        u = ubuf[t % 2, 0]
        u2 = u * u
        v = u * (GC + (GC * 0.044715) * u2)
        th = jnp.tanh(v)
        cdf = 0.5 + 0.5 * th
        acts[rows, cols] = (u * cdf).astype(BF)
        slope = cdf + (0.5 - 0.5 * (th * th)) * (u * (GC + (3 * 0.044715 * GC) * u2))
        dus[rows, cols] = (ubuf[t % 2, 1] * slope).astype(BF)

    for t in range(-1, len(blocks)):
        if t + 1 < len(blocks):
            first(t + 1)
        if t >= 0:
            second(t)


def kernel(
    factor, tok_ref, up_ref, gain1_ref, gain2_ref, wa, wp, we, wrt,
    out_ref, o_one, o_two, o_attn, o_proj, o_exp, o_red,
    rx, rg, rbx, rbg, rbo, ob, wat, wpt, wet, wr, gain1, gain2,
    s_red, s_exp, s_proj, s_two, s_attn, s_one,
    probs, packed, vnat, h1s, n1s, r1s, mixes, dy1s, dmixs, deltas, sbuf, dbuf, ebuf, acts, dus, ubuf,
    a_parts, a_got, a_cross, a_final, b_parts, b_got, b_cross, b_final,
    x_send, x_recv, g_send, g_recv, x_own, g_own, y_send, y_recv, y_own, zx_send, zx_recv, zg_send, zg_recv, zo_send, zo_recv, a_sems, b_sems,
):
    a, b, first, second = place()
    barrier = pltpu.get_barrier_semaphore()
    for dx, dy in SHIFTS:
        for sign in (-1, 1):
            pl.semaphore_signal(
                barrier, inc=1, device_id=neighbour(sign * dx, sign * dy), device_id_type=MESH
            )

    for dx, dy in RELAYS:
        for sign in (-1, 1):
            pl.semaphore_signal(
                barrier, inc=1, device_id=neighbour(sign * dx, sign * dy), device_id_type=MESH
            )

    def greet(r, carry):
        pl.semaphore_signal(
            barrier, inc=1, device_id=device(lax.rem(first + r, GROUP), second), device_id_type=MESH
        )
        pl.semaphore_signal(
            barrier, inc=1, device_id=device(first, lax.rem(second + r, GROUP)), device_id_type=MESH
        )
        return carry

    lax.fori_loop(1, GROUP, greet, 0)
    for part in range(PARTS):
        own_in(tok_ref, rx, x_own, part).start()
        own_in(up_ref, rg, g_own, part).start()
    wat[...] = flip(wa[...])
    wpt[...] = flip(wp[...])
    wet[...] = flip(we[...])
    wr[...] = flip(wrt[...])
    gain1[...] = jnp.broadcast_to(gain1_ref[...], (128, D)).T
    gain2[...] = jnp.broadcast_to(gain2_ref[...], (128, D)).T
    s_red[...] = jnp.zeros_like(s_red)
    s_exp[...] = jnp.zeros_like(s_exp)
    s_proj[...] = jnp.zeros_like(s_proj)
    s_two[...] = jnp.zeros_like(s_two)
    s_attn[...] = jnp.zeros_like(s_attn)
    s_one[...] = jnp.zeros_like(s_one)

    pl.semaphore_wait(barrier, 2 * len(SHIFTS) + 2 * len(RELAYS) + 2 * (GROUP - 1))
    edge = lax.rem(b, 4) == 0
    relay = lax.rem(b, 4) == 3
    for src, dst, via, send, recv, via_recv in (
        (tok_ref, rx, rbx, x_send, x_recv, zx_recv),
        (up_ref, rg, rbg, g_send, g_recv, zg_recv),
    ):
        for part in range(PARTS):

            @pl.when(edge)
            def _():
                relay_in(src, via, send, via_recv, part).start()

            @pl.when(jnp.logical_not(edge))
            def _():
                halo_in(src, dst, send, recv, part, 0).start()

            for k in (1, 2):
                halo_in(src, dst, send, recv, part, k).start()

    def forward(part, first_array):
        @pl.when(relay)
        def _():
            if first_array:
                relay_in(tok_ref, rbx, x_send, zx_recv, part).wait_recv()
                relay_on(rbx, rx, zx_send, x_recv, part).start()
            else:
                relay_in(up_ref, rbg, g_send, zg_recv, part).wait_recv()
                relay_on(rbg, rg, zg_send, g_recv, part).start()

    def attend(w, carry):
        for at, part, first_array in FORWARD:

            @pl.when(w == at)
            def _(part=part, first_array=first_array):
                forward(part, first_array)

        for part in range(PARTS):

            @pl.when(w == READY[part])
            def _(part=part):
                own_in(tok_ref, rx, x_own, part).wait()
                for k in range(3):
                    halo_in(tok_ref, rx, x_send, x_recv, part, k).wait_recv()

        lo, hi = offsets(w)
        x = load_window(rx, lo, hi)
        h1f, n1, r1 = norm_cols(x, wide(gain1[...]))
        h1 = h1f.astype(BF)
        h1s[w] = h1
        n1s[w] = n1
        r1s[w] = jnp.broadcast_to(r1, (8, TOK))
        pk = nn(wat[...], h1).astype(BF)
        packed[w] = pk
        qt, vt = pk[0:96], pk[192:288]
        kn = pk[96:192].T
        vnat[w] = vt.T
        mixed_f = attn_forward(w, qt, kn, vt, probs, sbuf)
        mixes[w] = mixed_f
        return carry

    lax.fori_loop(0, 8, attend, 0)

    def mlp(w, carry):
        for part in range(PARTS):

            @pl.when(w == READY[part])
            def _(part=part):
                own_in(up_ref, rg, g_own, part).wait()
                for k in range(3):
                    halo_in(up_ref, rg, g_send, g_recv, part, k).wait_recv()

        lo, hi = offsets(w)
        x = load_window(rx, lo, hi)
        mixed_f = mixes[w]
        mixed = mixed_f.astype(BF)
        branch = nn(wpt[...], mixed).astype(BF)
        y1 = (x + branch.astype(F32)).astype(BF).astype(F32)
        gain_b = wide(gain2[...])
        h2f, n2, r2 = norm_cols(y1, gain_b)
        h2 = h2f.astype(BF)
        gf = load_window(rg, lo, hi)
        gb = gf.astype(BF)
        mlp_middle(h2, gb, wet, wr, acts, dus, ubuf)
        s_red[...] += nt(gb, acts[...])
        du = dus[...]
        s_exp[...] += nt(h2, du)
        dh2 = nn(we[...], du)
        s_two[...] += fold(dh2 * n2)
        dy1 = gf + norm_back(dh2, n2, r2, gain_b)
        dy1s[w] = dy1
        da = dy1.astype(BF)
        s_proj[...] += nt(mixed, da)
        dmix = nn(wp[...], da).astype(BF)
        dmixs[w] = dmix
        prod = dmix.astype(F32) * mixed_f
        rows = [jnp.sum(prod[HD * h : HD * (h + 1)], axis=0, keepdims=True) for h in range(HEADS)]
        deltas[w] = jnp.concatenate(rows + [jnp.zeros((8 - HEADS, TOK), F32)], axis=0)
        return carry

    lax.fori_loop(0, 8, mlp, 0)

    two = jnp.broadcast_to(jnp.sum(s_two[...], axis=1, keepdims=True), (D, 32))
    tail = jnp.concatenate([s_proj[...], two], axis=1)
    tiles = [s_red[:, 0:128], s_red[:, 128:256], s_red[:, 256:384]]
    tiles += [s_exp[:, 0:128], s_exp[:, 128:256], s_exp[:, 256:384], tail]
    for j in range(8):
        for i in range(2):
            rows = slice(ROWS_A * i, ROWS_A * (i + 1))
            a_parts[2 * j + i] = tiles[j][rows] if j < 7 else jnp.zeros((ROWS_A, 128), F32)
    reduce_start(a_parts, a_got, a_sems)

    relay_back = lax.rem(b, 4) == 0

    def pass_on(i):
        @pl.when(relay_back)
        def _():
            relay_out(ob, rbo, y_send, zo_recv, piece(i), i).wait_recv()
            relay_done(rbo, out_ref, zo_send, y_recv, piece(i)).start()

    def back(w, carry):
        @pl.when(w > 0)
        def _():
            cols = pl.ds(pl.multiple_of((2 * w - 1) * CH, 128), 2 * CH)
            send_out(ob, out_ref, y_send, y_recv, y_own, rbo, zo_recv, cols, w - 1)

        @pl.when(jnp.logical_and(w > 2, relay_back))
        def _():
            cols = pl.ds(pl.multiple_of((2 * w - 5) * CH, 128), 2 * CH)
            relay_out(ob, rbo, y_send, zo_recv, cols, w - 3).wait_recv()
            relay_done(rbo, out_ref, zo_send, y_recv, cols).start()

        @pl.when(w == 6)
        def _():
            reduce_middle(a_got, a_cross, a_sems, factor)

        lo, hi = offsets(w)
        pk = packed[w]
        qt, kt = pk[0:96], pk[96:192]
        vn = vnat[w]
        dmix = dmixs[w]
        delta = deltas[w]
        dpk = attn_backward(w, qt, kt, vn, dmix, delta, probs, dbuf, ebuf)
        s_attn[...] += nt(h1s[w], dpk)
        dh1 = nn(wa[...], dpk).astype(BF).astype(F32)
        n1 = n1s[w]
        s_one[...] += fold(dh1 * n1)
        r1 = r1s[w][0:1]
        store_window(ob, lo, hi, dy1s[w] + norm_back(dh1, n1, r1, wide(gain1[...])))
        return carry

    lax.fori_loop(0, 8, back, 0)

    for j in range(2):
        for i in range(6):
            b_parts[6 * j + i] = s_attn[16 * i : 16 * i + 16, 128 * j : 128 * j + 128]
    rest = s_attn[:, 256:288]
    rest = jnp.concatenate([rest[24 * i : 24 * i + 24] for i in range(4)], axis=1)
    one = jnp.broadcast_to(jnp.sum(s_one[...], axis=1, keepdims=True), (D, 128)).T[0:8]
    rest = jnp.concatenate([rest, jnp.concatenate([one, jnp.zeros((8, 32), F32)], axis=1)], axis=0)
    b_parts[12] = rest[0:16]
    b_parts[13] = rest[16:32]
    for i in range(14, GROUP):
        b_parts[i] = jnp.zeros((ROWS_B, 128), F32)
    reduce_start(b_parts, b_got, b_sems)
    for i in (7, 8):
        send_out(ob, out_ref, y_send, y_recv, y_own, rbo, zo_recv, piece(i), i)
    pass_on(5)
    pass_on(6)
    reduce_last(a_cross, a_final, a_sems)
    pass_on(7)
    pass_on(8)
    reduce_middle(b_got, b_cross, b_sems, factor)
    reduce_end(a_final, a_sems)
    fa = [jnp.concatenate([a_final[2 * j], a_final[2 * j + 1]], axis=0) for j in range(7)]
    o_red[...] = jnp.concatenate(fa[0:3], axis=1)
    o_exp[...] = jnp.concatenate(fa[3:6], axis=1)
    o_proj[...] = fa[6][:, 0:96]
    o_two[...] = fa[6].T[96:97]
    reduce_last(b_cross, b_final, b_sems)
    for part in range(PARTS):
        for k in range(3):
            halo_in(tok_ref, rx, x_send, x_recv, part, k).wait_send()
            halo_in(up_ref, rg, g_send, g_recv, part, k).wait_send()

    everything = pl.ds(0, 16 * CH)

    @pl.when(relay)
    def _():
        for part in range(PARTS):
            relay_on(rbx, rx, zx_send, x_recv, part).wait_send()
            relay_on(rbg, rg, zg_send, g_recv, part).wait_send()

    @pl.when(relay_back)
    def _():
        relay_done(rbo, out_ref, zo_send, y_recv, everything).wait_send()

    own_out(ob, out_ref, y_own, everything).wait()
    for k in range(3):
        done = halo_out(ob, out_ref, y_send, y_recv, k, everything)
        done.wait_send()
        done.wait_recv()
    reduce_end(b_final, b_sems)
    fb = [jnp.concatenate([b_final[6 * j + i] for i in range(6)], axis=0) for j in range(2)]
    rest = jnp.concatenate([b_final[12], b_final[13]], axis=0)
    last = jnp.concatenate([rest[0:24, 32 * i : 32 * i + 32] for i in range(4)], axis=0)
    o_attn[...] = jnp.concatenate(fb + [last], axis=1)
    o_one[...] = rest[24:25, 0:96]


def finish(*refs):
    for src, dst in zip(refs[:7], refs[7:]):
        dst[...] = src[...]


def local(tokens, upstream, gain_one, gain_two, attn_weight, proj_weight, expand_weight, reduce_weight):
    count = tokens.shape[0] * tokens.shape[1] * (tokens.shape[2] // D)
    factor = 1.0 / math.sqrt(count * lax.axis_size("gx") * lax.axis_size("gy"))
    vm = pl.BlockSpec(memory_space=pltpu.VMEM)
    hbm = pl.BlockSpec(memory_space=pl.ANY)
    shape = jax.ShapeDtypeStruct
    dma = pltpu.SemaphoreType.DMA
    outs = pl.pallas_call(
        functools.partial(kernel, factor),
        in_specs=[hbm, hbm] + [vm] * 6,
        out_specs=[hbm] + [vm] * 6,
        out_shape=[
            shape((8, 8, 6144), BF),
            shape((1, D), F32),
            shape((1, D), F32),
            shape((D, 3 * D), F32),
            shape((D, D), F32),
            shape((D, HID), F32),
            shape((D, HID), F32),
        ],
        scratch_shapes=[
            pltpu.VMEM((8, 8, 6144), BF),
            pltpu.VMEM((8, 8, 6144), BF),
            pltpu.VMEM((8, 8, 6144), BF),
            pltpu.VMEM((8, 8, 6144), BF),
            pltpu.VMEM((8, 8, 6144), BF),
            pltpu.VMEM((8, 8, 6144), BF),
            pltpu.VMEM((3 * D, D), BF),
            pltpu.VMEM((D, D), BF),
            pltpu.VMEM((HID, D), BF),
            pltpu.VMEM((HID, D), BF),
            pltpu.VMEM((D, 128), F32),
            pltpu.VMEM((D, 128), F32),
            pltpu.VMEM((D, HID), F32),
            pltpu.VMEM((D, HID), F32),
            pltpu.VMEM((D, D), F32),
            pltpu.VMEM((D, 128), F32),
            pltpu.VMEM((D, 3 * D), F32),
            pltpu.VMEM((D, 128), F32),
            pltpu.VMEM((24, TOK, TOK), BF),
            pltpu.VMEM((8, 3 * D, TOK), BF),
            pltpu.VMEM((8, TOK, D), BF),
            pltpu.VMEM((8, D, TOK), BF),
            pltpu.VMEM((8, D, TOK), F32),
            pltpu.VMEM((8, 8, TOK), F32),
            pltpu.VMEM((8, D, TOK), F32),
            pltpu.VMEM((8, D, TOK), F32),
            pltpu.VMEM((8, D, TOK), BF),
            pltpu.VMEM((8, 8, TOK), F32),
            pltpu.VMEM((3, TOK, 256), F32),
            pltpu.VMEM((2, 256, 256), F32),
            pltpu.VMEM((2, 256, 256), BF),
            pltpu.VMEM((HID, TOK), BF),
            pltpu.VMEM((HID, TOK), BF),
            pltpu.VMEM((2, 2, 64, 256), F32),
        ]
        + [pltpu.VMEM((GROUP, ROWS_A, 128), F32)] * 4
        + [pltpu.VMEM((GROUP, ROWS_B, 128), F32)] * 4
        + [dma((PARTS, 3))] * 4
        + [dma((PARTS,))] * 2
        + [dma((3,))] * 2
        + [dma]
        + [dma((PARTS,))] * 4
        + [dma, dma((9,)), dma((2, 3)), dma((2, 3))],
        compiler_params=pltpu.CompilerParams(
            vmem_limit_bytes=56 * 1024 * 1024, collective_id=0, has_side_effects=True
        ),
        name="block_backward",
    )(
        tokens, upstream, gain_one.reshape(1, D), gain_two.reshape(1, D),
        attn_weight, proj_weight, expand_weight, reduce_weight.T,
    )
    grad, one, two, attn, proj, exp, red = pl.pallas_call(
        finish,
        in_specs=[vm] * 7,
        out_specs=[vm] * 7,
        out_shape=[shape(v.shape, v.dtype) for v in outs],
        name="finish",
    )(*outs)
    return (grad, one.reshape(D), two.reshape(D), attn, proj, exp, red.T)


def solution(mesh):
    return jax.shard_map(
        local,
        mesh=mesh,
        in_specs=(P("gx", "gy", None), P("gx", "gy", None), P(), P(), P(), P(), P(), P()),
        out_specs=(P("gx", "gy", None), P(), P(), P(), P(), P(), P()),
        check_vma=False,
    )
```

```python
import functools
import math

import jax
import jax.numpy as jnp
from jax import lax
from jax.experimental import pallas as pl
from jax.experimental.pallas import tpu as pltpu
from jax.sharding import PartitionSpec as P

D = 96
HEADS = 3
HD = 32
WIN = 8
HID = 384
TOK = 512
CH = 384
EPS = 1e-05
F32 = jnp.float32
BF = jnp.bfloat16
SCALE = HD**-0.5
LOG2E = 1.4426950408889634
GC = math.sqrt(2.0 / math.pi)


def nn(a, b):
    return lax.dot_general(a, b, (((1,), (0,)), ((), ())), preferred_element_type=F32)


def nt(a, b):
    return lax.dot_general(a, b, (((1,), (1,)), ((), ())), preferred_element_type=F32)


def wide(col):
    return jnp.concatenate([col] * (TOK // 128), axis=1)


def fold(v):
    return v[:, 0:128] + v[:, 128:256] + v[:, 256:384] + v[:, 384:512]


def mean0(v):
    return jnp.sum(v, axis=0, keepdims=True) * (1.0 / D)


def norm_cols(v, gain):
    c = v - mean0(v)
    r = lax.rsqrt(mean0(c * c) + EPS)
    n = c * r
    return n * gain, n, r


def norm_back(dh, n, r, gain):
    e = dh * gain
    return r * (e - mean0(e) - n * mean0(e * n))


def flip(v):
    return v.astype(F32).T.astype(v.dtype)


def load_window(ref, lo, hi):
    a = ref[:, :, pl.ds(lo, CH)].astype(F32).reshape(64, CH)
    b = ref[:, :, pl.ds(hi, CH)].astype(F32).reshape(64, CH)
    t = jnp.concatenate([a, b], axis=0).T
    return jnp.concatenate([t[0:96], t[96:192], t[192:288], t[288:384]], axis=1)


def store_window(ref, lo, hi, v):
    t = jnp.concatenate([v[:, 128 * i : 128 * (i + 1)] for i in range(4)], axis=0).T
    ref[:, :, pl.ds(lo, CH)] = t[0:64].reshape(8, 8, CH).astype(BF)
    ref[:, :, pl.ds(hi, CH)] = t[64:128].reshape(8, 8, CH).astype(BF)


def only_head(v, h):
    zero = jnp.zeros((HD, v.shape[1]), v.dtype)
    rows = [v[HD * h : HD * (h + 1)] if i == h else zero for i in range(HEADS)]
    return jnp.concatenate(rows, axis=0)


def offsets(w):
    lo = pl.multiple_of((2 * w + 1) * CH, 128)
    hi = pl.multiple_of(lax.rem(2 * w + 2, 16) * CH, 128)
    return lo, hi


MESH = pl.DeviceIdType.MESH
NGX, NGY = 32, 8
GROUP = 16
SHIFTS = ((1, 1), (0, 1), (1, 0))
RELAYS = ((1, -3), (0, 4))
CUTS = (0, 3 * CH, 7 * CH, 13 * CH, 16 * CH)
PARTS = 4
READY = (0, 1, 3, 6)
FORWARD = (
    (0, 0, True), (1, 1, True), (2, 2, True), (3, 3, True),
    (3, 0, False), (4, 1, False), (5, 2, False), (6, 3, False),
)
ROWS_A, ROWS_B = 48, 16


def half(flag):
    return pl.ds(4, 4) if flag else pl.ds(0, 4)


def place():
    a, b = lax.axis_index("gx"), lax.axis_index("gy")
    first = (a // 8) * 4 + lax.rem(b, 4)
    second = (b // 4) * 8 + lax.rem(a, 8)
    return a, b, first, second


def device(first, second):
    return ((first // 4) * 8 + lax.rem(second, 8), (second // 8) * 4 + lax.rem(first, 4))


def neighbour(dx, dy):
    a, b = lax.axis_index("gx"), lax.axis_index("gy")
    return (lax.rem(a + dx + NGX, NGX), lax.rem(b + dy + NGY, NGY))


def remote(src, dst, send, recv, where):
    return pltpu.make_async_remote_copy(
        src_ref=src, dst_ref=dst, send_sem=send, recv_sem=recv, device_id=where, device_id_type=MESH
    )


def halo_in(src, dst, send, recv, part, k):
    dx, dy = SHIFTS[k]
    cols = pl.ds(CUTS[part], CUTS[part + 1] - CUTS[part])
    return remote(
        src.at[half(not dx), half(not dy), cols], dst.at[half(dx), half(dy), cols],
        send.at[part, k], recv.at[part, k], neighbour(-dx, -dy),
    )


def relay_in(src, dst, send, recv, part):
    cols = pl.ds(CUTS[part], CUTS[part + 1] - CUTS[part])
    return remote(
        src.at[half(0), half(0), cols], dst.at[half(1), half(1), cols],
        send.at[part, 0], recv.at[part], neighbour(-1, 3),
    )


def relay_on(src, dst, send, recv, part):
    box = (half(1), half(1), pl.ds(CUTS[part], CUTS[part + 1] - CUTS[part]))
    return remote(src.at[box], dst.at[box], send.at[part], recv.at[part, 0], neighbour(0, 4))


def piece(i):
    if i < 7:
        return pl.ds((2 * i + 1) * CH, 2 * CH)
    return pl.ds(15 * CH if i == 7 else 0, CH)


def relay_out(src, dst, send, recv, cols, i):
    box = (half(1), half(1), cols)
    return remote(src.at[box], dst.at[box], send.at[0], recv.at[i], neighbour(1, -3))


def relay_done(src, dst, send, recv, cols):
    return remote(
        src.at[half(1), half(1), cols], dst.at[half(0), half(0), cols],
        send, recv.at[0], neighbour(0, 4),
    )


def own_in(src, dst, sem, part):
    cols = pl.ds(CUTS[part], CUTS[part + 1] - CUTS[part])
    return pltpu.make_async_copy(
        src.at[half(1), half(1), cols], dst.at[half(0), half(0), cols], sem.at[part]
    )


def halo_out(src, dst, send, recv, k, cols):
    dx, dy = SHIFTS[k]
    return remote(
        src.at[half(dx), half(dy), cols], dst.at[half(not dx), half(not dy), cols],
        send.at[k], recv.at[k], neighbour(dx, dy),
    )


def own_out(src, dst, sem, cols):
    return pltpu.make_async_copy(
        src.at[half(0), half(0), cols], dst.at[half(1), half(1), cols], sem
    )


def send_out(src, dst, send, recv, sem, via, via_recv, cols, i):
    edge = lax.rem(lax.axis_index("gy"), 4) == 3

    @pl.when(edge)
    def _():
        relay_out(src, via, send, via_recv, cols, i).start()

    @pl.when(jnp.logical_not(edge))
    def _():
        halo_out(src, dst, send, recv, 0, cols).start()

    for k in (1, 2):
        halo_out(src, dst, send, recv, k, cols).start()
    own_out(src, dst, sem, cols).start()


def spread(src_of, dst, slot, send, recv, along_first):
    a, b, first, second = place()
    mine = first if along_first else second

    def step(r, carry):
        to = lax.rem(mine + r, GROUP)
        where = device(to, second) if along_first else device(first, to)
        remote(src_of(to), dst.at[slot], send, recv, where).start()
        return carry

    lax.fori_loop(1, GROUP, step, 0)


def settle(buf, send, recv):
    most = buf.at[pl.ds(0, GROUP - 1)]
    done = remote(most, most, send, recv, neighbour(1, 0))
    done.wait_recv()
    done.wait_send()


def total(buf):
    acc = buf[0]
    for i in range(1, GROUP):
        acc = acc + buf[i]
    return acc


def reduce_start(parts, got, sems):
    a, b, first, second = place()
    got[first] = parts[first]
    spread(lambda to: parts.at[to], got, first, sems.at[0, 0], sems.at[1, 0], True)


def reduce_middle(got, cross, sems, factor):
    a, b, first, second = place()
    settle(got, sems.at[0, 0], sems.at[1, 0])
    cross[second] = total(got) * factor
    spread(lambda to: cross.at[second], cross, second, sems.at[0, 1], sems.at[1, 1], False)


def reduce_last(cross, final, sems):
    a, b, first, second = place()
    settle(cross, sems.at[0, 1], sems.at[1, 1])
    final[first] = total(cross)
    spread(lambda to: final.at[first], final, first, sems.at[0, 2], sems.at[1, 2], True)


def reduce_end(final, sems):
    settle(final, sems.at[0, 2], sems.at[1, 2])


def attn_forward(w, qt, kn, vt, probs, sbuf):
    units = [(h, c) for h in range(HEADS) for c in range(2)]
    top, mixed = {}, {}
    sums = {}

    def rows_of(j):
        return slice(64 * j, 64 * (j + 1))

    def score(t, j):
        h, c = units[t]
        s = nn(kn[rows_of(j)], heads[h][:, 256 * c : 256 * (c + 1)])
        sbuf[t % 3, rows_of(j), :] = s
        m = jnp.max(s.reshape(64 // 8, 8, 256), axis=0)
        top[t] = m if j == 0 else jnp.maximum(top[t], m)

    def power(t, j, m):
        e = jnp.exp2((sbuf[t % 3, rows_of(j), :] - m) * (SCALE * LOG2E))
        sbuf[t % 3, rows_of(j), :] = e
        part = jnp.sum(e.reshape(64 // 8, 8, 256), axis=0)
        sums[t] = part if j == 0 else sums[t] + part

    def weigh(t, j, inv):
        h, c = units[t]
        p = (sbuf[t % 3, rows_of(j), :] * inv).astype(BF)
        probs[w * HEADS + h, rows_of(j), 256 * c : 256 * (c + 1)] = p

    def mix(t):
        h, c = units[t]
        p = probs[w * HEADS + h, :, 256 * c : 256 * (c + 1)]
        mixed[t] = nn(vt[HD * h : HD * (h + 1)], p)

    heads = [only_head(qt, h) for h in range(HEADS)]
    n, steps = len(units), TOK // 64
    for t in range(-1, n + 1):
        if 0 <= t < n:
            m = jnp.max(top[t], axis=0, keepdims=True)
        if t >= 1:
            inv = 1.0 / jnp.sum(sums[t - 1], axis=0, keepdims=True)
        for j in range(steps):
            if t + 1 < n:
                score(t + 1, j)
            if 0 <= t < n:
                power(t, j, m)
            if t >= 1:
                weigh(t - 1, j, inv)
        if t >= 1:
            mix(t - 1)
    out = [jnp.concatenate([mixed[2 * h], mixed[2 * h + 1]], axis=1) for h in range(HEADS)]
    return jnp.concatenate(out, axis=0)


def attn_backward(w, qt, kt, vn, dmix, delta, probs, dbuf, ebuf):
    units = [(h, k, c) for k in range(2) for h in range(HEADS) for c in range(2)]
    dq, dk, dv = {}, {}, {}
    heads = [only_head(dmix, h) for h in range(HEADS)]

    def tile(i):
        return slice(256 * i, 256 * (i + 1))

    def grow(table, key, v):
        table[key] = v if key not in table else table[key] + v

    def first(t, j):
        h, k, c = units[t]
        rows = slice(256 * k + 128 * j, 256 * k + 128 * (j + 1))
        dbuf[t % 2, 128 * j : 128 * (j + 1), :] = nn(vn[rows], heads[h][:, tile(c)])

    def middle(t, j):
        h, k, c = units[t]
        rows = slice(256 * k + 128 * j, 256 * k + 128 * (j + 1))
        p = probs[w * HEADS + h, rows, tile(c)].astype(F32)
        dp = dbuf[t % 2, 128 * j : 128 * (j + 1), :]
        ds = p * (dp - delta[h : h + 1, tile(c)]) * SCALE
        ebuf[t % 2, 128 * j : 128 * (j + 1), :] = ds.astype(BF)

    def last(t, j):
        h, k, c = units[t]
        rows = slice(HD * h, HD * (h + 1))
        ds = ebuf[t % 2]
        if j == 0:
            grow(dq, (h, c), nn(kt[rows, tile(k)], ds))
        elif j == 1:
            grow(dk, (h, k), nt(qt[rows, tile(c)], ds))
        elif j == 2:
            grow(dv, (h, k), nt(dmix[rows, tile(c)], probs[w * HEADS + h, tile(k), tile(c)]))

    n = len(units)
    for t in range(-1, n + 1):
        for j in range(max(256 // 128, 3)):
            if t + 1 < n and j < 256 // 128:
                first(t + 1, j)
            if t >= 1:
                last(t - 1, j)
            if 0 <= t < n and j < 256 // 128:
                middle(t, j)
    parts = [jnp.concatenate([v[h, 0], v[h, 1]], axis=1) for v in (dq, dk, dv) for h in range(HEADS)]
    return jnp.concatenate(parts, axis=0).astype(BF)


def mlp_middle(h2, gb, wet, wr, acts, dus, ubuf):
    blocks = [(r, c) for c in range(TOK // 256) for r in range(HID // 64)]

    def box(t):
        r, c = blocks[t]
        return slice(64 * r, 64 * (r + 1)), slice(256 * c, 256 * (c + 1))

    def first(t):
        rows, cols = box(t)
        ubuf[t % 2, 0] = nn(wet[rows, :], h2[:, cols])
        ubuf[t % 2, 1] = nn(wr[rows, :], gb[:, cols])

    def second(t):
        rows, cols = box(t)
        u = ubuf[t % 2, 0]
        u2 = u * u
        v = u * (GC + (GC * 0.044715) * u2)
        th = jnp.tanh(v)
        cdf = 0.5 + 0.5 * th
        acts[rows, cols] = (u * cdf).astype(BF)
        slope = cdf + (0.5 - 0.5 * (th * th)) * (u * (GC + (3 * 0.044715 * GC) * u2))
        dus[rows, cols] = (ubuf[t % 2, 1] * slope).astype(BF)

    for t in range(-1, len(blocks)):
        if t + 1 < len(blocks):
            first(t + 1)
        if t >= 0:
            second(t)


def kernel(
    factor, tok_ref, up_ref, gain1_ref, gain2_ref, wa, wp, we, wrt,
    out_ref, o_one, o_two, o_attn, o_proj, o_exp, o_red,
    rx, rg, rbx, rbg, rbo, ob, wat, wpt, wet, wr, gain1, gain2,
    s_red, s_exp, s_proj, s_two, s_attn, s_one,
    probs, packed, vnat, h1s, n1s, r1s, mixes, dy1s, dmixs, deltas, sbuf, dbuf, ebuf, acts, dus, ubuf,
    a_parts, a_got, a_cross, a_final, b_parts, b_got, b_cross, b_final,
    x_send, x_recv, g_send, g_recv, x_own, g_own, y_send, y_recv, y_own, zx_send, zx_recv, zg_send, zg_recv, zo_send, zo_recv, a_sems, b_sems,
):
    a, b, first, second = place()
    barrier = pltpu.get_barrier_semaphore()
    for dx, dy in SHIFTS:
        for sign in (-1, 1):
            pl.semaphore_signal(
                barrier, inc=1, device_id=neighbour(sign * dx, sign * dy), device_id_type=MESH
            )

    for dx, dy in RELAYS:
        for sign in (-1, 1):
            pl.semaphore_signal(
                barrier, inc=1, device_id=neighbour(sign * dx, sign * dy), device_id_type=MESH
            )

    def greet(r, carry):
        pl.semaphore_signal(
            barrier, inc=1, device_id=device(lax.rem(first + r, GROUP), second), device_id_type=MESH
        )
        pl.semaphore_signal(
            barrier, inc=1, device_id=device(first, lax.rem(second + r, GROUP)), device_id_type=MESH
        )
        return carry

    lax.fori_loop(1, GROUP, greet, 0)
    for part in range(PARTS):
        own_in(tok_ref, rx, x_own, part).start()
        own_in(up_ref, rg, g_own, part).start()
    wat[...] = flip(wa[...])
    wpt[...] = flip(wp[...])
    wet[...] = flip(we[...])
    wr[...] = flip(wrt[...])
    gain1[...] = jnp.broadcast_to(gain1_ref[...], (128, D)).T
    gain2[...] = jnp.broadcast_to(gain2_ref[...], (128, D)).T
    s_red[...] = jnp.zeros_like(s_red)
    s_exp[...] = jnp.zeros_like(s_exp)
    s_proj[...] = jnp.zeros_like(s_proj)
    s_two[...] = jnp.zeros_like(s_two)
    s_attn[...] = jnp.zeros_like(s_attn)
    s_one[...] = jnp.zeros_like(s_one)

    pl.semaphore_wait(barrier, 2 * len(SHIFTS) + 2 * len(RELAYS) + 2 * (GROUP - 1))
    edge = lax.rem(b, 4) == 0
    relay = lax.rem(b, 4) == 3
    for src, dst, via, send, recv, via_recv in (
        (tok_ref, rx, rbx, x_send, x_recv, zx_recv),
        (up_ref, rg, rbg, g_send, g_recv, zg_recv),
    ):
        for part in range(PARTS):

            @pl.when(edge)
            def _():
                relay_in(src, via, send, via_recv, part).start()

            @pl.when(jnp.logical_not(edge))
            def _():
                halo_in(src, dst, send, recv, part, 0).start()

            for k in (1, 2):
                halo_in(src, dst, send, recv, part, k).start()

    def forward(part, first_array):
        @pl.when(relay)
        def _():
            if first_array:
                relay_in(tok_ref, rbx, x_send, zx_recv, part).wait_recv()
                relay_on(rbx, rx, zx_send, x_recv, part).start()
            else:
                relay_in(up_ref, rbg, g_send, zg_recv, part).wait_recv()
                relay_on(rbg, rg, zg_send, g_recv, part).start()

    def attend(w, carry):
        for at, part, first_array in FORWARD:

            @pl.when(w == at)
            def _(part=part, first_array=first_array):
                forward(part, first_array)

        for part in range(PARTS):

            @pl.when(w == READY[part])
            def _(part=part):
                own_in(tok_ref, rx, x_own, part).wait()
                for k in range(3):
                    halo_in(tok_ref, rx, x_send, x_recv, part, k).wait_recv()

        lo, hi = offsets(w)
        x = load_window(rx, lo, hi)
        h1f, n1, r1 = norm_cols(x, wide(gain1[...]))
        h1 = h1f.astype(BF)
        h1s[w] = h1
        n1s[w] = n1
        r1s[w] = jnp.broadcast_to(r1, (8, TOK))
        pk = nn(wat[...], h1).astype(BF)
        packed[w] = pk
        qt, vt = pk[0:96], pk[192:288]
        kn = pk[96:192].T
        vnat[w] = vt.T
        mixed_f = attn_forward(w, qt, kn, vt, probs, sbuf)
        mixes[w] = mixed_f
        return carry

    lax.fori_loop(0, 8, attend, 0)

    def mlp(w, carry):
        for part in range(PARTS):

            @pl.when(w == READY[part])
            def _(part=part):
                own_in(up_ref, rg, g_own, part).wait()
                for k in range(3):
                    halo_in(up_ref, rg, g_send, g_recv, part, k).wait_recv()

        lo, hi = offsets(w)
        x = load_window(rx, lo, hi)
        mixed_f = mixes[w]
        mixed = mixed_f.astype(BF)
        branch = nn(wpt[...], mixed).astype(BF)
        y1 = (x + branch.astype(F32)).astype(BF).astype(F32)
        gain_b = wide(gain2[...])
        h2f, n2, r2 = norm_cols(y1, gain_b)
        h2 = h2f.astype(BF)
        gf = load_window(rg, lo, hi)
        gb = gf.astype(BF)
        mlp_middle(h2, gb, wet, wr, acts, dus, ubuf)
        s_red[...] += nt(gb, acts[...])
        du = dus[...]
        s_exp[...] += nt(h2, du)
        dh2 = nn(we[...], du)
        s_two[...] += fold(dh2 * n2)
        dy1 = gf + norm_back(dh2, n2, r2, gain_b)
        dy1s[w] = dy1
        da = dy1.astype(BF)
        s_proj[...] += nt(mixed, da)
        dmix = nn(wp[...], da).astype(BF)
        dmixs[w] = dmix
        prod = dmix.astype(F32) * mixed_f
        rows = [jnp.sum(prod[HD * h : HD * (h + 1)], axis=0, keepdims=True) for h in range(HEADS)]
        deltas[w] = jnp.concatenate(rows + [jnp.zeros((8 - HEADS, TOK), F32)], axis=0)
        return carry

    lax.fori_loop(0, 8, mlp, 0)

    two = jnp.broadcast_to(jnp.sum(s_two[...], axis=1, keepdims=True), (D, 32))
    tail = jnp.concatenate([s_proj[...], two], axis=1)
    tiles = [s_red[:, 0:128], s_red[:, 128:256], s_red[:, 256:384]]
    tiles += [s_exp[:, 0:128], s_exp[:, 128:256], s_exp[:, 256:384], tail]
    for j in range(8):
        for i in range(2):
            rows = slice(ROWS_A * i, ROWS_A * (i + 1))
            a_parts[2 * j + i] = tiles[j][rows] if j < 7 else jnp.zeros((ROWS_A, 128), F32)
    reduce_start(a_parts, a_got, a_sems)

    relay_back = lax.rem(b, 4) == 0

    def pass_on(i):
        @pl.when(relay_back)
        def _():
            relay_out(ob, rbo, y_send, zo_recv, piece(i), i).wait_recv()
            relay_done(rbo, out_ref, zo_send, y_recv, piece(i)).start()

    def back(w, carry):
        @pl.when(w > 0)
        def _():
            cols = pl.ds(pl.multiple_of((2 * w - 1) * CH, 128), 2 * CH)
            send_out(ob, out_ref, y_send, y_recv, y_own, rbo, zo_recv, cols, w - 1)

        @pl.when(jnp.logical_and(w > 2, relay_back))
        def _():
            cols = pl.ds(pl.multiple_of((2 * w - 5) * CH, 128), 2 * CH)
            relay_out(ob, rbo, y_send, zo_recv, cols, w - 3).wait_recv()
            relay_done(rbo, out_ref, zo_send, y_recv, cols).start()

        @pl.when(w == 5)
        def _():
            reduce_middle(a_got, a_cross, a_sems, factor)

        lo, hi = offsets(w)
        pk = packed[w]
        qt, kt = pk[0:96], pk[96:192]
        vn = vnat[w]
        dmix = dmixs[w]
        delta = deltas[w]
        dpk = attn_backward(w, qt, kt, vn, dmix, delta, probs, dbuf, ebuf)
        s_attn[...] += nt(h1s[w], dpk)
        dh1 = nn(wa[...], dpk).astype(BF).astype(F32)
        n1 = n1s[w]
        s_one[...] += fold(dh1 * n1)
        r1 = r1s[w][0:1]
        store_window(ob, lo, hi, dy1s[w] + norm_back(dh1, n1, r1, wide(gain1[...])))
        return carry

    lax.fori_loop(0, 8, back, 0)

    for j in range(2):
        for i in range(6):
            b_parts[6 * j + i] = s_attn[16 * i : 16 * i + 16, 128 * j : 128 * j + 128]
    rest = s_attn[:, 256:288]
    rest = jnp.concatenate([rest[24 * i : 24 * i + 24] for i in range(4)], axis=1)
    one = jnp.broadcast_to(jnp.sum(s_one[...], axis=1, keepdims=True), (D, 128)).T[0:8]
    rest = jnp.concatenate([rest, jnp.concatenate([one, jnp.zeros((8, 32), F32)], axis=1)], axis=0)
    b_parts[12] = rest[0:16]
    b_parts[13] = rest[16:32]
    for i in range(14, GROUP):
        b_parts[i] = jnp.zeros((ROWS_B, 128), F32)
    reduce_start(b_parts, b_got, b_sems)
    for i in (7, 8):
        send_out(ob, out_ref, y_send, y_recv, y_own, rbo, zo_recv, piece(i), i)
    for i in (5, 6, 7, 8):
        pass_on(i)
    reduce_middle(b_got, b_cross, b_sems, factor)
    reduce_last(a_cross, a_final, a_sems)
    reduce_last(b_cross, b_final, b_sems)
    reduce_end(a_final, a_sems)
    fa = [jnp.concatenate([a_final[2 * j], a_final[2 * j + 1]], axis=0) for j in range(7)]
    o_red[...] = jnp.concatenate(fa[0:3], axis=1)
    o_exp[...] = jnp.concatenate(fa[3:6], axis=1)
    o_proj[...] = fa[6][:, 0:96]
    o_two[...] = fa[6].T[96:97]
    for part in range(PARTS):
        for k in range(3):
            halo_in(tok_ref, rx, x_send, x_recv, part, k).wait_send()
            halo_in(up_ref, rg, g_send, g_recv, part, k).wait_send()

    everything = pl.ds(0, 16 * CH)

    @pl.when(relay)
    def _():
        for part in range(PARTS):
            relay_on(rbx, rx, zx_send, x_recv, part).wait_send()
            relay_on(rbg, rg, zg_send, g_recv, part).wait_send()

    @pl.when(relay_back)
    def _():
        relay_done(rbo, out_ref, zo_send, y_recv, everything).wait_send()

    own_out(ob, out_ref, y_own, everything).wait()
    for k in range(3):
        done = halo_out(ob, out_ref, y_send, y_recv, k, everything)
        done.wait_send()
        done.wait_recv()
    reduce_end(b_final, b_sems)
    fb = [jnp.concatenate([b_final[6 * j + i] for i in range(6)], axis=0) for j in range(2)]
    rest = jnp.concatenate([b_final[12], b_final[13]], axis=0)
    last = jnp.concatenate([rest[0:24, 32 * i : 32 * i + 32] for i in range(4)], axis=0)
    o_attn[...] = jnp.concatenate(fb + [last], axis=1)
    o_one[...] = rest[24:25, 0:96]


def finish(*refs):
    for src, dst in zip(refs[:7], refs[7:]):
        dst[...] = src[...]


def local(tokens, upstream, gain_one, gain_two, attn_weight, proj_weight, expand_weight, reduce_weight):
    count = tokens.shape[0] * tokens.shape[1] * (tokens.shape[2] // D)
    factor = 1.0 / math.sqrt(count * lax.axis_size("gx") * lax.axis_size("gy"))
    vm = pl.BlockSpec(memory_space=pltpu.VMEM)
    hbm = pl.BlockSpec(memory_space=pl.ANY)
    shape = jax.ShapeDtypeStruct
    dma = pltpu.SemaphoreType.DMA
    outs = pl.pallas_call(
        functools.partial(kernel, factor),
        in_specs=[hbm, hbm] + [vm] * 6,
        out_specs=[hbm] + [vm] * 6,
        out_shape=[
            shape((8, 8, 6144), BF),
            shape((1, D), F32),
            shape((1, D), F32),
            shape((D, 3 * D), F32),
            shape((D, D), F32),
            shape((D, HID), F32),
            shape((D, HID), F32),
        ],
        scratch_shapes=[
            pltpu.VMEM((8, 8, 6144), BF),
            pltpu.VMEM((8, 8, 6144), BF),
            pltpu.VMEM((8, 8, 6144), BF),
            pltpu.VMEM((8, 8, 6144), BF),
            pltpu.VMEM((8, 8, 6144), BF),
            pltpu.VMEM((8, 8, 6144), BF),
            pltpu.VMEM((3 * D, D), BF),
            pltpu.VMEM((D, D), BF),
            pltpu.VMEM((HID, D), BF),
            pltpu.VMEM((HID, D), BF),
            pltpu.VMEM((D, 128), F32),
            pltpu.VMEM((D, 128), F32),
            pltpu.VMEM((D, HID), F32),
            pltpu.VMEM((D, HID), F32),
            pltpu.VMEM((D, D), F32),
            pltpu.VMEM((D, 128), F32),
            pltpu.VMEM((D, 3 * D), F32),
            pltpu.VMEM((D, 128), F32),
            pltpu.VMEM((24, TOK, TOK), BF),
            pltpu.VMEM((8, 3 * D, TOK), BF),
            pltpu.VMEM((8, TOK, D), BF),
            pltpu.VMEM((8, D, TOK), BF),
            pltpu.VMEM((8, D, TOK), F32),
            pltpu.VMEM((8, 8, TOK), F32),
            pltpu.VMEM((8, D, TOK), F32),
            pltpu.VMEM((8, D, TOK), F32),
            pltpu.VMEM((8, D, TOK), BF),
            pltpu.VMEM((8, 8, TOK), F32),
            pltpu.VMEM((3, TOK, 256), F32),
            pltpu.VMEM((2, 256, 256), F32),
            pltpu.VMEM((2, 256, 256), BF),
            pltpu.VMEM((HID, TOK), BF),
            pltpu.VMEM((HID, TOK), BF),
            pltpu.VMEM((2, 2, 64, 256), F32),
        ]
        + [pltpu.VMEM((GROUP, ROWS_A, 128), F32)] * 4
        + [pltpu.VMEM((GROUP, ROWS_B, 128), F32)] * 4
        + [dma((PARTS, 3))] * 4
        + [dma((PARTS,))] * 2
        + [dma((3,))] * 2
        + [dma]
        + [dma((PARTS,))] * 4
        + [dma, dma((9,)), dma((2, 3)), dma((2, 3))],
        compiler_params=pltpu.CompilerParams(
            vmem_limit_bytes=56 * 1024 * 1024, collective_id=0, has_side_effects=True
        ),
        name="block_backward",
    )(
        tokens, upstream, gain_one.reshape(1, D), gain_two.reshape(1, D),
        attn_weight, proj_weight, expand_weight, reduce_weight.T,
    )
    grad, one, two, attn, proj, exp, red = pl.pallas_call(
        finish,
        in_specs=[vm] * 7,
        out_specs=[vm] * 7,
        out_shape=[shape(v.shape, v.dtype) for v in outs],
        name="finish",
    )(*outs)
    return (grad, one.reshape(D), two.reshape(D), attn, proj, exp, red.T)


def solution(mesh):
    return jax.shard_map(
        local,
        mesh=mesh,
        in_specs=(P("gx", "gy", None), P("gx", "gy", None), P(), P(), P(), P(), P(), P()),
        out_specs=(P("gx", "gy", None), P(), P(), P(), P(), P(), P()),
        check_vma=False,
    )
```

```python
import functools
import math

import jax
import jax.numpy as jnp
from jax import lax
from jax.experimental import pallas as pl
from jax.experimental.pallas import tpu as pltpu
from jax.sharding import PartitionSpec as P

D = 96
HEADS = 3
HD = 32
WIN = 8
HID = 384
TOK = 512
CH = 384
EPS = 1e-05
F32 = jnp.float32
BF = jnp.bfloat16
SCALE = HD**-0.5
LOG2E = 1.4426950408889634
GC = math.sqrt(2.0 / math.pi)


def nn(a, b):
    return lax.dot_general(a, b, (((1,), (0,)), ((), ())), preferred_element_type=F32)


def nt(a, b):
    return lax.dot_general(a, b, (((1,), (1,)), ((), ())), preferred_element_type=F32)


def wide(col):
    return jnp.concatenate([col] * (TOK // 128), axis=1)


def fold(v):
    return v[:, 0:128] + v[:, 128:256] + v[:, 256:384] + v[:, 384:512]


def mean0(v):
    return jnp.sum(v, axis=0, keepdims=True) * (1.0 / D)


def norm_cols(v, gain):
    c = v - mean0(v)
    r = lax.rsqrt(mean0(c * c) + EPS)
    n = c * r
    return n * gain, n, r


def norm_back(dh, n, r, gain):
    e = dh * gain
    return r * (e - mean0(e) - n * mean0(e * n))


def flip(v):
    return v.astype(F32).T.astype(v.dtype)


def load_window(ref, lo, hi):
    a = ref[:, :, pl.ds(lo, CH)].astype(F32).reshape(64, CH)
    b = ref[:, :, pl.ds(hi, CH)].astype(F32).reshape(64, CH)
    t = jnp.concatenate([a, b], axis=0).T
    return jnp.concatenate([t[0:96], t[96:192], t[192:288], t[288:384]], axis=1)


def store_window(ref, lo, hi, v):
    t = jnp.concatenate([v[:, 128 * i : 128 * (i + 1)] for i in range(4)], axis=0).T
    ref[:, :, pl.ds(lo, CH)] = t[0:64].reshape(8, 8, CH).astype(BF)
    ref[:, :, pl.ds(hi, CH)] = t[64:128].reshape(8, 8, CH).astype(BF)


def only_head(v, h):
    zero = jnp.zeros((HD, v.shape[1]), v.dtype)
    rows = [v[HD * h : HD * (h + 1)] if i == h else zero for i in range(HEADS)]
    return jnp.concatenate(rows, axis=0)


def offsets(w):
    lo = pl.multiple_of((2 * w + 1) * CH, 128)
    hi = pl.multiple_of(lax.rem(2 * w + 2, 16) * CH, 128)
    return lo, hi


MESH = pl.DeviceIdType.MESH
NGX, NGY = 32, 8
GROUP = 16
SHIFTS = ((1, 1), (0, 1), (1, 0))
RELAYS = ((1, -3), (0, 4))
CUTS = (0, 3 * CH, 7 * CH, 13 * CH, 16 * CH)
PARTS = 4
READY = (0, 1, 3, 6)
FORWARD = (
    (0, 0, True), (1, 1, True), (2, 2, True), (3, 3, True),
    (3, 0, False), (4, 1, False), (5, 2, False), (6, 3, False),
)
ROWS_A, ROWS_B = 48, 16


def half(flag):
    return pl.ds(4, 4) if flag else pl.ds(0, 4)


def place():
    a, b = lax.axis_index("gx"), lax.axis_index("gy")
    first = (a // 8) * 4 + lax.rem(b, 4)
    second = (b // 4) * 8 + lax.rem(a, 8)
    return a, b, first, second


def device(first, second):
    return ((first // 4) * 8 + lax.rem(second, 8), (second // 8) * 4 + lax.rem(first, 4))


def neighbour(dx, dy):
    a, b = lax.axis_index("gx"), lax.axis_index("gy")
    return (lax.rem(a + dx + NGX, NGX), lax.rem(b + dy + NGY, NGY))


def remote(src, dst, send, recv, where):
    return pltpu.make_async_remote_copy(
        src_ref=src, dst_ref=dst, send_sem=send, recv_sem=recv, device_id=where, device_id_type=MESH
    )


def halo_in(src, dst, send, recv, part, k):
    dx, dy = SHIFTS[k]
    cols = pl.ds(CUTS[part], CUTS[part + 1] - CUTS[part])
    return remote(
        src.at[half(not dx), half(not dy), cols], dst.at[half(dx), half(dy), cols],
        send.at[part, k], recv.at[part, k], neighbour(-dx, -dy),
    )


def relay_in(src, dst, send, recv, part):
    cols = pl.ds(CUTS[part], CUTS[part + 1] - CUTS[part])
    return remote(
        src.at[half(0), half(0), cols], dst.at[half(1), half(1), cols],
        send.at[part, 0], recv.at[part], neighbour(-1, 3),
    )


def relay_on(src, dst, send, recv, part):
    box = (half(1), half(1), pl.ds(CUTS[part], CUTS[part + 1] - CUTS[part]))
    return remote(src.at[box], dst.at[box], send.at[part], recv.at[part, 0], neighbour(0, 4))


def piece(i):
    if i < 7:
        return pl.ds((2 * i + 1) * CH, 2 * CH)
    return pl.ds(15 * CH if i == 7 else 0, CH)


def relay_out(src, dst, send, recv, cols, i):
    box = (half(1), half(1), cols)
    return remote(src.at[box], dst.at[box], send.at[0], recv.at[i], neighbour(1, -3))


def relay_done(src, dst, send, recv, cols):
    return remote(
        src.at[half(1), half(1), cols], dst.at[half(0), half(0), cols],
        send, recv.at[0], neighbour(0, 4),
    )


def own_in(src, dst, sem, part):
    cols = pl.ds(CUTS[part], CUTS[part + 1] - CUTS[part])
    return pltpu.make_async_copy(
        src.at[half(1), half(1), cols], dst.at[half(0), half(0), cols], sem.at[part]
    )


def halo_out(src, dst, send, recv, k, cols):
    dx, dy = SHIFTS[k]
    return remote(
        src.at[half(dx), half(dy), cols], dst.at[half(not dx), half(not dy), cols],
        send.at[k], recv.at[k], neighbour(dx, dy),
    )


def own_out(src, dst, sem, cols):
    return pltpu.make_async_copy(
        src.at[half(0), half(0), cols], dst.at[half(1), half(1), cols], sem
    )


def send_out(src, dst, send, recv, sem, via, via_recv, cols, i):
    edge = lax.rem(lax.axis_index("gy"), 4) == 3

    @pl.when(edge)
    def _():
        relay_out(src, via, send, via_recv, cols, i).start()

    @pl.when(jnp.logical_not(edge))
    def _():
        halo_out(src, dst, send, recv, 0, cols).start()

    for k in (1, 2):
        halo_out(src, dst, send, recv, k, cols).start()
    own_out(src, dst, sem, cols).start()


def spread(src_of, dst, slot, send, recv, along_first):
    a, b, first, second = place()
    mine = first if along_first else second

    def step(r, carry):
        to = lax.rem(mine + r, GROUP)
        where = device(to, second) if along_first else device(first, to)
        remote(src_of(to), dst.at[slot], send, recv, where).start()
        return carry

    lax.fori_loop(1, GROUP, step, 0)


def settle(buf, send, recv):
    most = buf.at[pl.ds(0, GROUP - 1)]
    done = remote(most, most, send, recv, neighbour(1, 0))
    done.wait_recv()
    done.wait_send()


def total(buf):
    acc = buf[0]
    for i in range(1, GROUP):
        acc = acc + buf[i]
    return acc


def reduce_start(parts, got, sems):
    a, b, first, second = place()
    got[first] = parts[first]
    spread(lambda to: parts.at[to], got, first, sems.at[0, 0], sems.at[1, 0], True)


def reduce_middle(got, cross, sems, factor):
    a, b, first, second = place()
    settle(got, sems.at[0, 0], sems.at[1, 0])
    cross[second] = total(got) * factor
    spread(lambda to: cross.at[second], cross, second, sems.at[0, 1], sems.at[1, 1], False)


def reduce_last(cross, final, sems):
    a, b, first, second = place()
    settle(cross, sems.at[0, 1], sems.at[1, 1])
    final[first] = total(cross)
    spread(lambda to: final.at[first], final, first, sems.at[0, 2], sems.at[1, 2], True)


def reduce_end(final, sems):
    settle(final, sems.at[0, 2], sems.at[1, 2])


def attn_forward(w, qt, kn, vt, probs, sbuf):
    units = [(h, c) for h in range(HEADS) for c in range(2)]
    top, mixed = {}, {}
    sums = {}

    def rows_of(j):
        return slice(64 * j, 64 * (j + 1))

    def score(t, j):
        h, c = units[t]
        s = nn(kn[rows_of(j)], heads[h][:, 256 * c : 256 * (c + 1)])
        sbuf[t % 3, rows_of(j), :] = s
        m = jnp.max(s.reshape(64 // 8, 8, 256), axis=0)
        top[t] = m if j == 0 else jnp.maximum(top[t], m)

    def power(t, j, m):
        e = jnp.exp2((sbuf[t % 3, rows_of(j), :] - m) * (SCALE * LOG2E))
        sbuf[t % 3, rows_of(j), :] = e
        part = jnp.sum(e.reshape(64 // 8, 8, 256), axis=0)
        sums[t] = part if j == 0 else sums[t] + part

    def weigh(t, j, inv):
        h, c = units[t]
        p = (sbuf[t % 3, rows_of(j), :] * inv).astype(BF)
        probs[w * HEADS + h, rows_of(j), 256 * c : 256 * (c + 1)] = p

    def mix(t):
        h, c = units[t]
        p = probs[w * HEADS + h, :, 256 * c : 256 * (c + 1)]
        mixed[t] = nn(vt[HD * h : HD * (h + 1)], p)

    heads = [only_head(qt, h) for h in range(HEADS)]
    n, steps = len(units), TOK // 64
    for t in range(-1, n + 1):
        if 0 <= t < n:
            m = jnp.max(top[t], axis=0, keepdims=True)
        if t >= 1:
            inv = 1.0 / jnp.sum(sums[t - 1], axis=0, keepdims=True)
        for j in range(steps):
            if t + 1 < n:
                score(t + 1, j)
            if 0 <= t < n:
                power(t, j, m)
            if t >= 1:
                weigh(t - 1, j, inv)
        if t >= 1:
            mix(t - 1)
    out = [jnp.concatenate([mixed[2 * h], mixed[2 * h + 1]], axis=1) for h in range(HEADS)]
    return jnp.concatenate(out, axis=0)


def attn_backward(w, qt, kt, vn, dmix, delta, probs, dbuf, ebuf, extra):
    units = [(h, k, c) for k in range(2) for h in range(HEADS) for c in range(2)]
    dq, dk, dv = {}, {}, {}
    heads = [only_head(dmix, h) for h in range(HEADS)]

    def tile(i):
        return slice(256 * i, 256 * (i + 1))

    def grow(table, key, v):
        table[key] = v if key not in table else table[key] + v

    def first(t, j):
        h, k, c = units[t]
        rows = slice(256 * k + 128 * j, 256 * k + 128 * (j + 1))
        dbuf[t % 2, 128 * j : 128 * (j + 1), :] = nn(vn[rows], heads[h][:, tile(c)])

    def middle(t, j):
        h, k, c = units[t]
        rows = slice(256 * k + 128 * j, 256 * k + 128 * (j + 1))
        p = probs[w * HEADS + h, rows, tile(c)].astype(F32)
        dp = dbuf[t % 2, 128 * j : 128 * (j + 1), :]
        ds = p * (dp - delta[h : h + 1, tile(c)]) * SCALE
        ebuf[t % 2, 128 * j : 128 * (j + 1), :] = ds.astype(BF)

    def last(t, j):
        h, k, c = units[t]
        rows = slice(HD * h, HD * (h + 1))
        ds = ebuf[t % 2]
        if j == 0:
            grow(dq, (h, c), nn(kt[rows, tile(k)], ds))
        elif j == 1:
            grow(dk, (h, k), nt(qt[rows, tile(c)], ds))
        elif j == 2:
            grow(dv, (h, k), nt(dmix[rows, tile(c)], probs[w * HEADS + h, tile(k), tile(c)]))

    n = len(units)
    for t in range(-1, n + 1):
        for j in range(max(256 // 128, 3)):
            if t + 1 < n and j < 256 // 128:
                first(t + 1, j)
            if t >= 1:
                last(t - 1, j)
            if 0 <= t < n and j < 256 // 128:
                middle(t, j)
        if t in extra:
            extra[t]()
    parts = [jnp.concatenate([v[h, 0], v[h, 1]], axis=1) for v in (dq, dk, dv) for h in range(HEADS)]
    return jnp.concatenate(parts, axis=0).astype(BF)


def mlp_middle(h2, gb, wet, wr, acts, dus, ubuf):
    blocks = [(r, c) for c in range(TOK // 256) for r in range(HID // 64)]

    def box(t):
        r, c = blocks[t]
        return slice(64 * r, 64 * (r + 1)), slice(256 * c, 256 * (c + 1))

    def first(t):
        rows, cols = box(t)
        ubuf[t % 2, 0] = nn(wet[rows, :], h2[:, cols])
        ubuf[t % 2, 1] = nn(wr[rows, :], gb[:, cols])

    def second(t):
        rows, cols = box(t)
        u = ubuf[t % 2, 0]
        u2 = u * u
        v = u * (GC + (GC * 0.044715) * u2)
        th = jnp.tanh(v)
        cdf = 0.5 + 0.5 * th
        acts[rows, cols] = (u * cdf).astype(BF)
        slope = cdf + (0.5 - 0.5 * (th * th)) * (u * (GC + (3 * 0.044715 * GC) * u2))
        dus[rows, cols] = (ubuf[t % 2, 1] * slope).astype(BF)

    for t in range(-1, len(blocks)):
        if t + 1 < len(blocks):
            first(t + 1)
        if t >= 0:
            second(t)


def kernel(
    factor, tok_ref, up_ref, gain1_ref, gain2_ref, wa, wp, we, wrt,
    out_ref, o_one, o_two, o_attn, o_proj, o_exp, o_red,
    rx, rg, rbx, rbg, rbo, ob, wat, wpt, wet, wr, gain1, gain2,
    s_red, s_exp, s_proj, s_two, s_attn, s_one,
    probs, packed, vnat, h1s, n1s, r1s, mixes, dy1s, dmixs, deltas, dpks, sbuf, dbuf, ebuf, acts, dus, ubuf,
    a_parts, a_got, a_cross, a_final, b_parts, b_got, b_cross, b_final,
    x_send, x_recv, g_send, g_recv, x_own, g_own, y_send, y_recv, y_own, zx_send, zx_recv, zg_send, zg_recv, zo_send, zo_recv, a_sems, b_sems,
):
    a, b, first, second = place()
    barrier = pltpu.get_barrier_semaphore()
    for dx, dy in SHIFTS:
        for sign in (-1, 1):
            pl.semaphore_signal(
                barrier, inc=1, device_id=neighbour(sign * dx, sign * dy), device_id_type=MESH
            )

    for dx, dy in RELAYS:
        for sign in (-1, 1):
            pl.semaphore_signal(
                barrier, inc=1, device_id=neighbour(sign * dx, sign * dy), device_id_type=MESH
            )

    def greet(r, carry):
        pl.semaphore_signal(
            barrier, inc=1, device_id=device(lax.rem(first + r, GROUP), second), device_id_type=MESH
        )
        pl.semaphore_signal(
            barrier, inc=1, device_id=device(first, lax.rem(second + r, GROUP)), device_id_type=MESH
        )
        return carry

    lax.fori_loop(1, GROUP, greet, 0)
    for part in range(PARTS):
        own_in(tok_ref, rx, x_own, part).start()
        own_in(up_ref, rg, g_own, part).start()
    wat[...] = flip(wa[...])
    wpt[...] = flip(wp[...])
    wet[...] = flip(we[...])
    wr[...] = flip(wrt[...])
    gain1[...] = jnp.broadcast_to(gain1_ref[...], (128, D)).T
    gain2[...] = jnp.broadcast_to(gain2_ref[...], (128, D)).T
    s_red[...] = jnp.zeros_like(s_red)
    s_exp[...] = jnp.zeros_like(s_exp)
    s_proj[...] = jnp.zeros_like(s_proj)
    s_two[...] = jnp.zeros_like(s_two)
    s_attn[...] = jnp.zeros_like(s_attn)
    s_one[...] = jnp.zeros_like(s_one)

    pl.semaphore_wait(barrier, 2 * len(SHIFTS) + 2 * len(RELAYS) + 2 * (GROUP - 1))
    edge = lax.rem(b, 4) == 0
    relay = lax.rem(b, 4) == 3
    for src, dst, via, send, recv, via_recv in (
        (tok_ref, rx, rbx, x_send, x_recv, zx_recv),
        (up_ref, rg, rbg, g_send, g_recv, zg_recv),
    ):
        for part in range(PARTS):

            @pl.when(edge)
            def _():
                relay_in(src, via, send, via_recv, part).start()

            @pl.when(jnp.logical_not(edge))
            def _():
                halo_in(src, dst, send, recv, part, 0).start()

            for k in (1, 2):
                halo_in(src, dst, send, recv, part, k).start()

    def forward(part, first_array):
        @pl.when(relay)
        def _():
            if first_array:
                relay_in(tok_ref, rbx, x_send, zx_recv, part).wait_recv()
                relay_on(rbx, rx, zx_send, x_recv, part).start()
            else:
                relay_in(up_ref, rbg, g_send, zg_recv, part).wait_recv()
                relay_on(rbg, rg, zg_send, g_recv, part).start()

    def attend(w, carry):
        for at, part, first_array in FORWARD:

            @pl.when(w == at)
            def _(part=part, first_array=first_array):
                forward(part, first_array)

        for part in range(PARTS):

            @pl.when(w == READY[part])
            def _(part=part):
                own_in(tok_ref, rx, x_own, part).wait()
                for k in range(3):
                    halo_in(tok_ref, rx, x_send, x_recv, part, k).wait_recv()

        lo, hi = offsets(w)
        x = load_window(rx, lo, hi)
        h1f, n1, r1 = norm_cols(x, wide(gain1[...]))
        h1 = h1f.astype(BF)
        h1s[w] = h1
        n1s[w] = n1
        r1s[w] = jnp.broadcast_to(r1, (8, TOK))
        pk = nn(wat[...], h1).astype(BF)
        packed[w] = pk
        qt, vt = pk[0:96], pk[192:288]
        kn = pk[96:192].T
        vnat[w] = vt.T
        mixed_f = attn_forward(w, qt, kn, vt, probs, sbuf)
        mixes[w] = mixed_f
        return carry

    lax.fori_loop(0, 8, attend, 0)

    def mlp(w, carry):
        for part in range(PARTS):

            @pl.when(w == READY[part])
            def _(part=part):
                own_in(up_ref, rg, g_own, part).wait()
                for k in range(3):
                    halo_in(up_ref, rg, g_send, g_recv, part, k).wait_recv()

        lo, hi = offsets(w)
        x = load_window(rx, lo, hi)
        mixed_f = mixes[w]
        mixed = mixed_f.astype(BF)
        branch = nn(wpt[...], mixed).astype(BF)
        y1 = (x + branch.astype(F32)).astype(BF).astype(F32)
        gain_b = wide(gain2[...])
        h2f, n2, r2 = norm_cols(y1, gain_b)
        h2 = h2f.astype(BF)
        gf = load_window(rg, lo, hi)
        gb = gf.astype(BF)
        mlp_middle(h2, gb, wet, wr, acts, dus, ubuf)
        s_red[...] += nt(gb, acts[...])
        du = dus[...]
        s_exp[...] += nt(h2, du)
        dh2 = nn(we[...], du)
        s_two[...] += fold(dh2 * n2)
        dy1 = gf + norm_back(dh2, n2, r2, gain_b)
        dy1s[w] = dy1
        da = dy1.astype(BF)
        s_proj[...] += nt(mixed, da)
        dmix = nn(wp[...], da).astype(BF)
        dmixs[w] = dmix
        prod = dmix.astype(F32) * mixed_f
        rows = [jnp.sum(prod[HD * h : HD * (h + 1)], axis=0, keepdims=True) for h in range(HEADS)]
        deltas[w] = jnp.concatenate(rows + [jnp.zeros((8 - HEADS, TOK), F32)], axis=0)
        return carry

    lax.fori_loop(0, 8, mlp, 0)

    two = jnp.broadcast_to(jnp.sum(s_two[...], axis=1, keepdims=True), (D, 32))
    tail = jnp.concatenate([s_proj[...], two], axis=1)
    tiles = [s_red[:, 0:128], s_red[:, 128:256], s_red[:, 256:384]]
    tiles += [s_exp[:, 0:128], s_exp[:, 128:256], s_exp[:, 256:384], tail]
    for j in range(8):
        for i in range(2):
            rows = slice(ROWS_A * i, ROWS_A * (i + 1))
            a_parts[2 * j + i] = tiles[j][rows] if j < 7 else jnp.zeros((ROWS_A, 128), F32)
    reduce_start(a_parts, a_got, a_sems)

    relay_back = lax.rem(b, 4) == 0

    def pass_on(i):
        @pl.when(relay_back)
        def _():
            relay_out(ob, rbo, y_send, zo_recv, piece(i), i).wait_recv()
            relay_done(rbo, out_ref, zo_send, y_recv, piece(i)).start()

    def rest_of(v):
        held = {}

        def weights():
            s_attn[...] += nt(h1s[v], dpks[...])

        def product():
            held[0] = nn(wa[...], dpks[...]).astype(BF).astype(F32)

        def gains():
            s_one[...] += fold(held[0] * n1s[v])

        def result():
            lo, hi = offsets(v)
            part = norm_back(held[0], n1s[v], r1s[v][0:1], wide(gain1[...]))
            store_window(ob, lo, hi, dy1s[v] + part)

        return {0: weights, 2: product, 4: gains, 6: result}

    dpks[...] = jnp.zeros_like(dpks)

    def back(w, carry):
        @pl.when(w > 1)
        def _():
            cols = pl.ds(pl.multiple_of((2 * w - 3) * CH, 128), 2 * CH)
            send_out(ob, out_ref, y_send, y_recv, y_own, rbo, zo_recv, cols, w - 2)

        @pl.when(jnp.logical_and(w > 3, relay_back))
        def _():
            cols = pl.ds(pl.multiple_of((2 * w - 7) * CH, 128), 2 * CH)
            relay_out(ob, rbo, y_send, zo_recv, cols, w - 4).wait_recv()
            relay_done(rbo, out_ref, zo_send, y_recv, cols).start()

        @pl.when(w == 5)
        def _():
            reduce_middle(a_got, a_cross, a_sems, factor)

        pk = packed[w]
        dpk = attn_backward(
            w, pk[0:96], pk[96:192], vnat[w], dmixs[w], deltas[w], probs, dbuf, ebuf,
            rest_of(lax.rem(w + 7, 8)),
        )
        dpks[...] = dpk
        return carry

    lax.fori_loop(0, 8, back, 0)
    send_out(ob, out_ref, y_send, y_recv, y_own, rbo, zo_recv, piece(6), 6)
    steps = rest_of(7)
    for t in (0, 2, 4):
        steps[t]()

    for j in range(2):
        for i in range(6):
            b_parts[6 * j + i] = s_attn[16 * i : 16 * i + 16, 128 * j : 128 * j + 128]
    rest = s_attn[:, 256:288]
    rest = jnp.concatenate([rest[24 * i : 24 * i + 24] for i in range(4)], axis=1)
    one = jnp.broadcast_to(jnp.sum(s_one[...], axis=1, keepdims=True), (D, 128)).T[0:8]
    rest = jnp.concatenate([rest, jnp.concatenate([one, jnp.zeros((8, 32), F32)], axis=1)], axis=0)
    b_parts[12] = rest[0:16]
    b_parts[13] = rest[16:32]
    for i in range(14, GROUP):
        b_parts[i] = jnp.zeros((ROWS_B, 128), F32)
    reduce_start(b_parts, b_got, b_sems)
    steps[6]()
    for i in (4, 5):
        pass_on(i)
    for i in (7, 8):
        send_out(ob, out_ref, y_send, y_recv, y_own, rbo, zo_recv, piece(i), i)
    for i in (6, 7, 8):
        pass_on(i)
    reduce_middle(b_got, b_cross, b_sems, factor)
    reduce_last(a_cross, a_final, a_sems)
    reduce_last(b_cross, b_final, b_sems)
    reduce_end(a_final, a_sems)
    fa = [jnp.concatenate([a_final[2 * j], a_final[2 * j + 1]], axis=0) for j in range(7)]
    o_red[...] = jnp.concatenate(fa[0:3], axis=1)
    o_exp[...] = jnp.concatenate(fa[3:6], axis=1)
    o_proj[...] = fa[6][:, 0:96]
    o_two[...] = fa[6].T[96:97]
    for part in range(PARTS):
        for k in range(3):
            halo_in(tok_ref, rx, x_send, x_recv, part, k).wait_send()
            halo_in(up_ref, rg, g_send, g_recv, part, k).wait_send()

    everything = pl.ds(0, 16 * CH)

    @pl.when(relay)
    def _():
        for part in range(PARTS):
            relay_on(rbx, rx, zx_send, x_recv, part).wait_send()
            relay_on(rbg, rg, zg_send, g_recv, part).wait_send()

    @pl.when(relay_back)
    def _():
        relay_done(rbo, out_ref, zo_send, y_recv, everything).wait_send()

    own_out(ob, out_ref, y_own, everything).wait()
    for k in range(3):
        done = halo_out(ob, out_ref, y_send, y_recv, k, everything)
        done.wait_send()
        done.wait_recv()
    reduce_end(b_final, b_sems)
    fb = [jnp.concatenate([b_final[6 * j + i] for i in range(6)], axis=0) for j in range(2)]
    rest = jnp.concatenate([b_final[12], b_final[13]], axis=0)
    last = jnp.concatenate([rest[0:24, 32 * i : 32 * i + 32] for i in range(4)], axis=0)
    o_attn[...] = jnp.concatenate(fb + [last], axis=1)
    o_one[...] = rest[24:25, 0:96]


def finish(*refs):
    for src, dst in zip(refs[:7], refs[7:]):
        dst[...] = src[...]


def local(tokens, upstream, gain_one, gain_two, attn_weight, proj_weight, expand_weight, reduce_weight):
    count = tokens.shape[0] * tokens.shape[1] * (tokens.shape[2] // D)
    factor = 1.0 / math.sqrt(count * lax.axis_size("gx") * lax.axis_size("gy"))
    vm = pl.BlockSpec(memory_space=pltpu.VMEM)
    hbm = pl.BlockSpec(memory_space=pl.ANY)
    shape = jax.ShapeDtypeStruct
    dma = pltpu.SemaphoreType.DMA
    outs = pl.pallas_call(
        functools.partial(kernel, factor),
        in_specs=[hbm, hbm] + [vm] * 6,
        out_specs=[hbm] + [vm] * 6,
        out_shape=[
            shape((8, 8, 6144), BF),
            shape((1, D), F32),
            shape((1, D), F32),
            shape((D, 3 * D), F32),
            shape((D, D), F32),
            shape((D, HID), F32),
            shape((D, HID), F32),
        ],
        scratch_shapes=[
            pltpu.VMEM((8, 8, 6144), BF),
            pltpu.VMEM((8, 8, 6144), BF),
            pltpu.VMEM((8, 8, 6144), BF),
            pltpu.VMEM((8, 8, 6144), BF),
            pltpu.VMEM((8, 8, 6144), BF),
            pltpu.VMEM((8, 8, 6144), BF),
            pltpu.VMEM((3 * D, D), BF),
            pltpu.VMEM((D, D), BF),
            pltpu.VMEM((HID, D), BF),
            pltpu.VMEM((HID, D), BF),
            pltpu.VMEM((D, 128), F32),
            pltpu.VMEM((D, 128), F32),
            pltpu.VMEM((D, HID), F32),
            pltpu.VMEM((D, HID), F32),
            pltpu.VMEM((D, D), F32),
            pltpu.VMEM((D, 128), F32),
            pltpu.VMEM((D, 3 * D), F32),
            pltpu.VMEM((D, 128), F32),
            pltpu.VMEM((24, TOK, TOK), BF),
            pltpu.VMEM((8, 3 * D, TOK), BF),
            pltpu.VMEM((8, TOK, D), BF),
            pltpu.VMEM((8, D, TOK), BF),
            pltpu.VMEM((8, D, TOK), F32),
            pltpu.VMEM((8, 8, TOK), F32),
            pltpu.VMEM((8, D, TOK), F32),
            pltpu.VMEM((8, D, TOK), F32),
            pltpu.VMEM((8, D, TOK), BF),
            pltpu.VMEM((8, 8, TOK), F32),
            pltpu.VMEM((3 * D, TOK), BF),
            pltpu.VMEM((3, TOK, 256), F32),
            pltpu.VMEM((2, 256, 256), F32),
            pltpu.VMEM((2, 256, 256), BF),
            pltpu.VMEM((HID, TOK), BF),
            pltpu.VMEM((HID, TOK), BF),
            pltpu.VMEM((2, 2, 64, 256), F32),
        ]
        + [pltpu.VMEM((GROUP, ROWS_A, 128), F32)] * 4
        + [pltpu.VMEM((GROUP, ROWS_B, 128), F32)] * 4
        + [dma((PARTS, 3))] * 4
        + [dma((PARTS,))] * 2
        + [dma((3,))] * 2
        + [dma]
        + [dma((PARTS,))] * 4
        + [dma, dma((9,)), dma((2, 3)), dma((2, 3))],
        compiler_params=pltpu.CompilerParams(
            vmem_limit_bytes=56 * 1024 * 1024, collective_id=0, has_side_effects=True
        ),
        name="block_backward",
    )(
        tokens, upstream, gain_one.reshape(1, D), gain_two.reshape(1, D),
        attn_weight, proj_weight, expand_weight, reduce_weight.T,
    )
    grad, one, two, attn, proj, exp, red = pl.pallas_call(
        finish,
        in_specs=[vm] * 7,
        out_specs=[vm] * 7,
        out_shape=[shape(v.shape, v.dtype) for v in outs],
        name="finish",
    )(*outs)
    return (grad, one.reshape(D), two.reshape(D), attn, proj, exp, red.T)


def solution(mesh):
    return jax.shard_map(
        local,
        mesh=mesh,
        in_specs=(P("gx", "gy", None), P("gx", "gy", None), P(), P(), P(), P(), P(), P()),
        out_specs=(P("gx", "gy", None), P(), P(), P(), P(), P(), P()),
        check_vma=False,
    )
```
